256 devices in a mesh: cp: 32 (over z_lo, y, core), tp: 8 (over z_hi, x).
Axes of the slice: x: 4, y: 4, z: 8 (z_hi: 2, z_lo: 4; z = z_hi * 4 + z_lo), core: 2. Of those that a mesh axis runs over, the one named last changes fastest.
Arguments:
- tokens: bfloat16 [16384, 4096], P('cp', 'tp'), may hold values from -40 to 40
- span_ids: int32 [32, 2], P('cp'), may hold values from 0 to 63, as said below
- positions: int32 [16384], P('cp'), may hold values from 0 to 8191, as said below
- q_weight: bfloat16 [4096, 4096], P(None, 'tp'), may hold values from -0.09375 to 0.09375
- k_weight: bfloat16 [4096, 1024], P(None, 'tp'), may hold values from -0.09375 to 0.09375
- v_weight: bfloat16 [4096, 1024], P(None, 'tp'), may hold values from -0.09375 to 0.09375
- o_weight: bfloat16 [4096, 4096], P('tp'), may hold values from -0.09375 to 0.09375
Outputs:
- attended: bfloat16 [16384, 4096], P('cp', 'tp')
The draws below stay inside these ranges and needn't reach their ends.
Inputs may be any that keep to these rules, and one draw needn't show every extreme that they name: `span_ids`: row r names the two spans held by index r of cp: a span c and the span 64 - 1 - c, in either order; every span is named once. Span c covers the places c * (256) to (c + 1) * 256 - 1 of the sequence. `positions`: along the sequence (in the order of places given by span_ids) documents are runs of consecutive tokens; a position is 0 at a document's first token and rises by one up to its last, and the first place of the sequence has position 0.
All inputs are finite; a program needn't handle non-finite values.
Results may differ from the reference program's by a relative error of at most 0.014.
The reference program's roundings to bfloat16 on the way count: a program that leaves them out, or rounds other values in their place, can miss the bound.
Values may be sent and summed in bfloat16 or wider, within the bound.
A program may use at most 64 MiB of HBM per device.

```python
import jax
import jax.numpy as jnp
from jax import lax

D = 4096
HD = 128
HEADS_DEV = 4
TOK_DEV = 512
HEADS = 32
KV_HEADS = 8
TOKENS = 16384
N_CP = 32
N_TP = 8


def paired_table(key):
    rank_count = TOKENS // TOK_DEV
    shuffled = jax.random.permutation(jax.random.fold_in(key, 11), rank_count).astype(jnp.int32)
    swapped = jax.random.randint(jax.random.fold_in(key, 12), (rank_count,), 0, 2)
    low_span = shuffled
    high_span = (2 * rank_count - 1 - shuffled).astype(jnp.int32)
    first_span = jnp.where(swapped == 1, high_span, low_span)
    second_span = jnp.where(swapped == 1, low_span, high_span)
    return jnp.stack([first_span, second_span], axis=1).astype(jnp.int32)


def draw_span_ids(key, part):
    return paired_table(key)


def draw_positions(key, part):
    span_table = paired_table(key)
    half_rows = TOK_DEV // 2
    half_tokens = TOKENS // 2
    token_index = jnp.arange(TOKENS, dtype=jnp.int32)
    start_marks = jax.random.randint(jax.random.fold_in(key, 13), (TOKENS,), 0, max(TOKENS // 8, 2))
    marked = (start_marks == 0) & (token_index > half_tokens)
    starts = jnp.where(marked | (token_index == 0) | (token_index == half_tokens), token_index, 0)
    latest = lax.cummax(starts, axis=0)
    sequence_pos = (token_index - latest).astype(jnp.int32)
    offsets = jnp.arange(half_rows, dtype=jnp.int32)
    layout_index = (span_table[:, :, None] * half_rows + offsets[None, None, :]).reshape(TOKENS)
    return sequence_pos[layout_index].astype(jnp.int32)


def draw_tokens(key, part):
    normal_draw = jax.random.normal(jax.random.fold_in(key, 21), (TOKENS, D), jnp.float32)
    return jnp.clip(normal_draw, -40.0, 40.0).astype(jnp.bfloat16)


def block_scale(key, dims, cuts, smallest, largest):
    gain, own = 1.0, jax.random.fold_in(key, 6)
    for axis_at, blocks in cuts:
        steps = jnp.exp(jax.random.uniform(jax.random.fold_in(own, axis_at), (blocks,), jnp.float32, smallest / len(cuts), largest / len(cuts)))
        gain = gain * jnp.repeat(steps, dims[axis_at] // blocks).reshape([-1 if axis == axis_at else 1 for axis in range(len(dims))])
    return gain


def scatter_about(rng, dims, scale, reach, split=(), kind=jnp.bfloat16):
    factor_of = block_scale(rng, dims, split, -0.22, 0.18) if split else 1.0
    array = jax.random.normal(rng, dims, jnp.float32) * scale * factor_of
    return jnp.minimum(jnp.maximum(array, -reach), reach).astype(kind)


def setup_inputs(seed: int = 0) -> dict:
    streams_of = jax.random.split(jax.random.key(seed), 8)
    return {
        "tokens": draw_tokens(jax.random.fold_in(streams_of[7], 71), 0),
        "span_ids": draw_span_ids(jax.random.fold_in(streams_of[7], 71), 0),
        "positions": draw_positions(jax.random.fold_in(streams_of[7], 71), 0),
        "q_weight": scatter_about(streams_of[3], (D, HEADS * HD), D ** -0.5, 0.09375, ((1, 8),)),
        "k_weight": scatter_about(streams_of[4], (D, KV_HEADS * HD), D ** -0.5, 0.09375, ((1, 8),)),
        "v_weight": scatter_about(streams_of[5], (D, KV_HEADS * HD), D ** -0.5, 0.09375, ((1, 8),)),
        "o_weight": scatter_about(streams_of[6], (HEADS * HD, D), (HEADS * HD) ** -0.5, 0.09375, ((0, 8),)),
    }


theta_base = 500000.0


def rotate(vectors, positions):
    half_size = vectors.shape[-1] // 2
    exponent = jnp.arange(half_size, dtype=jnp.float32) * (2.0 / vectors.shape[-1])
    inverse_freq = theta_base ** (-exponent)
    angles = positions.astype(jnp.float32)[:, None] * inverse_freq[None, :]
    cosine = jnp.cos(angles)[:, None, :]
    sine_part = jnp.sin(angles)[:, None, :]
    lower_half = vectors[..., :half_size]
    upper_half = vectors[..., half_size:]
    return jnp.concatenate([lower_half * cosine - upper_half * sine_part, upper_half * cosine + lower_half * sine_part], axis=-1)


def reference(tokens, span_ids, positions, q_weight, k_weight, v_weight, o_weight):
    half_rows = TOK_DEV // 2
    scale_factor = HD ** -0.5
    queries = jnp.dot(tokens, q_weight, preferred_element_type=jnp.float32).reshape(TOKENS, HEADS, HD)
    keys_all = jnp.dot(tokens, k_weight, preferred_element_type=jnp.float32).reshape(TOKENS, KV_HEADS, HD)
    values_all = jnp.dot(tokens, v_weight, preferred_element_type=jnp.float32).astype(jnp.bfloat16).reshape(TOKENS, KV_HEADS, HD)
    queries = rotate(queries, positions).astype(jnp.bfloat16)
    keys_all = rotate(keys_all, positions).astype(jnp.bfloat16)
    offsets = jnp.arange(half_rows, dtype=jnp.int32)
    global_index = (span_ids[:, :, None] * half_rows + offsets[None, None, :]).reshape(TOKENS).astype(jnp.int32)
    doc_start = (global_index - positions).astype(jnp.int32)
    head_keys = jnp.transpose(keys_all, (1, 0, 2))
    head_values = jnp.transpose(values_all, (1, 0, 2))

    def one_block(inputs):
        block_queries, block_index, block_start = inputs
        grouped = jnp.transpose(block_queries.reshape(TOK_DEV, KV_HEADS, HEADS_DEV, HD), (1, 2, 0, 3))
        visible = (global_index[None, :] <= block_index[:, None]) & (global_index[None, :] >= block_start[:, None])

        def one_head(head_inputs):
            group_queries, keys_one, values_one = head_inputs
            scores = jnp.einsum("grd,kd->grk", group_queries.astype(jnp.float32), keys_one.astype(jnp.float32)) * scale_factor
            scores = jnp.where(visible[None], scores, -jnp.inf)
            row_max = jnp.max(scores, axis=-1, keepdims=True)
            weights = jnp.exp(scores - row_max)
            weight_sum = jnp.sum(weights, axis=-1, keepdims=True)
            rounded = lax.optimization_barrier(weights.astype(jnp.bfloat16)).astype(jnp.float32)
            mixture = jnp.einsum("grk,kd->grd", rounded, values_one.astype(jnp.float32))
            return mixture / weight_sum

        heads_out = lax.map(one_head, (grouped, head_keys, head_values))
        return jnp.transpose(heads_out, (2, 0, 1, 3)).reshape(TOK_DEV, HEADS * HD).astype(jnp.bfloat16)

    attended = lax.map(one_block, (queries.reshape(N_CP, TOK_DEV, HEADS, HD), global_index.reshape(N_CP, TOK_DEV), doc_start.reshape(N_CP, TOK_DEV)))
    attended = attended.reshape(TOKENS, N_TP, HEADS_DEV * HD)
    out_weight = o_weight.reshape(N_TP, HEADS_DEV * HD, D)
    summed = jnp.zeros((TOKENS, D), jnp.float32)
    for tp_rank in range(N_TP):
        partial_sum = jnp.dot(attended[:, tp_rank], out_weight[tp_rank], preferred_element_type=jnp.float32)
        summed = summed + lax.optimization_barrier(partial_sum.astype(jnp.bfloat16)).astype(jnp.float32)
    return summed.astype(jnp.bfloat16)
```

```python
import jax
import jax.numpy as jnp
from jax import lax
from jax.experimental import pallas as pl
from jax.experimental.pallas import tpu as pltpu
from jax.sharding import Mesh
from jax.sharding import PartitionSpec as P

HD = 128
TP = ("tp_0", "tp_1")
CP = ("cp_0", "cp_1", "cp_2")


theta_base = 500000.0
floor_score = -1e30


def sum_in_order(pieces, axes, order):
    inside = pieces.shape[1:]
    pieces = pieces.reshape(*(lax.axis_size(a) for a in axes), *inside)
    pieces = jnp.moveaxis(pieces, order, range(len(axes))).reshape(-1, *inside)
    for k in order:
        pieces = lax.psum_scatter(pieces, axes[k], scatter_dimension=0, tiled=True)
    return pieces[0]


def in_blocks(value, dim, length):
    shape = value.shape
    pieces = value.reshape(*shape[:dim], length, shape[dim] // length, *shape[dim + 1 :])
    return jnp.moveaxis(pieces, dim, 0)


def sum_by_axis(value, axes, order, dim):
    length = lax.axis_size(axes)
    return sum_in_order(in_blocks(value, dim, length), axes, order)


def rotate(vectors, positions):
    half_size = vectors.shape[-1] // 2
    exponent = jnp.arange(half_size, dtype=jnp.float32) * (2.0 / vectors.shape[-1])
    inverse_freq = theta_base ** (-exponent)
    angles = positions.astype(jnp.float32)[:, None] * inverse_freq[None, :]
    cosine = jnp.cos(angles)[:, None, :]
    sine_part = jnp.sin(angles)[:, None, :]
    lower_half = vectors[..., :half_size]
    upper_half = vectors[..., half_size:]
    return jnp.concatenate(
        [
            lower_half * cosine - upper_half * sine_part,
            upper_half * cosine + lower_half * sine_part,
        ],
        axis=-1,
    )


SPAN = 256
LOG2E = 1.4426950408889634


def attend_kernel(info, q_ref, kv_ref, start_ref, out_ref, top_ref, acc_ref):
    heads = q_ref.shape[1] // SPAN
    scale = LOG2E * HD**-0.5
    ones = jnp.ones((SPAN, HD), jnp.bfloat16)

    def block(half, span, masked, first):
        place = info[span]
        rank, part = place // 2, place % 2
        keys = kv_ref[rank, pl.ds(pl.multiple_of(part * SPAN, SPAN), SPAN), :]
        values = kv_ref[rank, pl.ds(pl.multiple_of((2 + part) * SPAN, SPAN), SPAN), :]
        values = jnp.concatenate([values, ones], axis=1)
        if masked:
            key = span * SPAN + lax.broadcasted_iota(jnp.int32, (SPAN, SPAN), 1)
            start = start_ref[half]
            seen = key >= jnp.concatenate([start, start], axis=1)
            if first:
                query = span * SPAN + lax.broadcasted_iota(jnp.int32, (SPAN, SPAN), 0)
                seen = seen & (key <= query)
        for head in range(heads):
            rows = slice(head * SPAN, (head + 1) * SPAN)
            score = lax.dot_general(
                q_ref[half, rows, :],
                keys,
                (((1,), (1,)), ((), ())),
                preferred_element_type=jnp.float32,
            )
            score = score * scale
            if masked:
                score = jnp.where(seen, score, floor_score)
            top = jnp.max(score, axis=1, keepdims=True)
            if first:
                weight = jnp.exp2(score - top)
                top_ref[rows, :] = jnp.broadcast_to(top, (SPAN, HD))
            else:
                before = top_ref[rows, :]
                now = jnp.maximum(before, top)
                weight = jnp.exp2(score - jnp.concatenate([now, now], axis=1))
                fade = jnp.exp2(before - now)
                top_ref[rows, :] = now
            mixed = jnp.dot(
                weight.astype(jnp.bfloat16), values, preferred_element_type=jnp.float32
            )
            if not first:
                mixed = mixed + acc_ref[rows, :] * jnp.concatenate([fade, fade], axis=1)
            acc_ref[rows, :] = mixed

    for half in range(2):
        own, low, clear = info[64 + half], info[66 + half], info[68 + half]
        block(half, own, True, True)
        lax.fori_loop(low, clear, lambda s, c: (block(half, s, True, False), c)[1], 0)
        lax.fori_loop(clear, own, lambda s, c: (block(half, s, False, False), c)[1], 0)
        for head in range(heads):
            rows = slice(head * SPAN, (head + 1) * SPAN)
            mixed = acc_ref[rows, :HD] / acc_ref[rows, HD:]
            out_ref[half * SPAN : (half + 1) * SPAN, head * HD : (head + 1) * HD] = mixed.astype(
                jnp.bfloat16
            )


def attend(info, queries, gathered, starts):
    vmem = pl.BlockSpec(memory_space=pltpu.VMEM)
    rows = queries.shape[1]
    heads = rows // SPAN
    return pl.pallas_call(
        attend_kernel,
        out_shape=jax.ShapeDtypeStruct((2 * SPAN, heads * HD), jnp.bfloat16),
        in_specs=[pl.BlockSpec(memory_space=pltpu.SMEM), vmem, vmem, vmem],
        out_specs=vmem,
        scratch_shapes=[
            pltpu.VMEM((rows, HD), jnp.float32),
            pltpu.VMEM((rows, 2 * HD), jnp.float32),
        ],
        compiler_params=pltpu.CompilerParams(vmem_limit_bytes=32 * 1024 * 1024),
        name="attend",
    )(info, queries, gathered, starts)


def plan(span_table, own, starts):
    blocks = jnp.arange(64, dtype=jnp.int32)
    where = jnp.sum(
        jnp.where(span_table.reshape(1, 64) == blocks[:, None], blocks[None, :], 0), axis=1
    )
    low = starts[:, 0] // SPAN
    clear = jnp.minimum((starts[:, -1] + SPAN - 1) // SPAN, own)
    return jnp.concatenate([where, own, low, clear, jnp.zeros(58, jnp.int32)])


def per_device(tokens, span_ids, positions, q_weight, k_weight, v_weight, o_weight):
    row_count = tokens.shape[0]
    half_rows = row_count // 2
    head_count = q_weight.shape[1] // HD
    weights_in = (q_weight, k_weight, v_weight)
    pieces = lax.all_gather(tokens, TP, axis=1, tiled=True)
    queries, keys_here, values_here = tuple(
        (jnp.dot(pieces, matrix, preferred_element_type=jnp.float32) for matrix in weights_in)
    )
    queries = rotate(queries.reshape(row_count, head_count, HD), positions).astype(jnp.bfloat16)
    queries = jnp.transpose(queries, (1, 0, 2))
    keys_here = (
        rotate(keys_here.reshape(row_count, 1, HD), positions)
        .reshape(row_count, HD)
        .astype(jnp.bfloat16)
    )
    values_here = values_here.astype(jnp.bfloat16)
    own = span_ids.reshape(2)
    own_rows = jnp.repeat(own.astype(jnp.bfloat16), 8)[:, None] * jnp.ones((1, HD), jnp.bfloat16)
    held = jnp.concatenate([keys_here, values_here, own_rows], axis=0)
    gathered = lax.all_gather(held, CP, axis=0, tiled=False)
    span_table = gathered[:, 2 * row_count :: 8, 0].astype(jnp.int32)
    offsets = jnp.arange(half_rows, dtype=jnp.int32)
    starts = own[:, None] * half_rows + offsets[None, :] - positions.reshape(2, half_rows)
    info = plan(span_table, own, starts)
    starts = jnp.broadcast_to(starts[:, :, None], (2, half_rows, HD))
    queries = queries.reshape(head_count, 2, half_rows, HD).transpose(1, 0, 2, 3)
    attention = attend(info, queries.reshape(2, head_count * half_rows, HD), gathered, starts)
    attention = attention.reshape(row_count, head_count, HD)
    out_weight = o_weight.reshape(head_count, HD, o_weight.shape[1])
    partial_sum = jnp.einsum(
        "rhd,hdn->rn", attention, out_weight, preferred_element_type=jnp.float32
    )
    return (
        sum_by_axis(partial_sum.astype(jnp.bfloat16), TP, (1, 0), 1)
        .astype(jnp.float32)
        .astype(jnp.bfloat16)
    )


def solution(mesh):
    split = Mesh(mesh.devices.reshape(4, 4, 2, 2, 4), ("cp_0", "cp_1", "cp_2", "tp_0", "tp_1"))
    placed = (P(CP, TP), P(CP, None), P(CP), P(None, TP), P(None, TP), P(None, TP), P(TP, None))
    return jax.shard_map(
        per_device, mesh=split, in_specs=placed, out_specs=P(CP, TP), check_vma=False
    )
```

```python
import jax
import jax.numpy as jnp
from jax import lax
from jax.experimental import pallas as pl
from jax.experimental.pallas import tpu as pltpu
from jax.sharding import Mesh
from jax.sharding import PartitionSpec as P

HD = 128
SPAN = 256
LOG2E = 1.4426950408889634
TP = ("tp_0", "tp_1")
CP = ("cp_0", "cp_1", "cp_2")


theta_base = 500000.0
floor_score = -1e30


MESH = pl.DeviceIdType.MESH
CHUNKS = 4
ROWS = 128
TAG = 2 * ROWS
BLOCK = TAG + 16


def shifted(x=0, y=0, z=0, row=0, other_core=False):
    place = {}
    if x:
        place["tp_1"] = lax.rem(lax.axis_index("tp_1") + x + 4, 4)
    if y:
        place["cp_1"] = lax.rem(lax.axis_index("cp_1") + y + 4, 4)
    if z:
        place["tp_0"] = 1 - lax.axis_index("tp_0")
    if row:
        place["cp_0"] = lax.rem(lax.axis_index("cp_0") + row, 4)
    if other_core:
        place["cp_2"] = 1 - lax.axis_index("cp_2")
    return place


def greet(peers):
    barrier = pltpu.get_barrier_semaphore()
    for peer in peers:
        pl.semaphore_signal(barrier, inc=1, device_id=peer, device_id_type=MESH)
    pl.semaphore_wait(barrier, len(peers))


def send(source, target, sems, index, peer):
    copy = pltpu.make_async_remote_copy(
        src_ref=source,
        dst_ref=target,
        send_sem=sems[0].at[index],
        recv_sem=sems[1].at[index],
        device_id=peer,
        device_id_type=MESH,
    )
    copy.start()
    return copy


def project_kernel(
    ids_ref,
    tokens_ref,
    wq_hbm,
    wk_hbm,
    wv_hbm,
    cos_ref,
    sin_ref,
    q_ref,
    kv_ref,
    wq_ref,
    wk_ref,
    wv_ref,
    held,
    weight_sem,
    token_send,
    token_recv,
    key_send,
    key_recv,
):
    x, zhi = lax.axis_index("tp_1"), lax.axis_index("tp_0")
    row, y, core = lax.axis_index("cp_0"), lax.axis_index("cp_1"), lax.axis_index("cp_2")
    loads = [
        pltpu.make_async_copy(a, b, weight_sem.at[i])
        for i, (a, b) in enumerate(((wk_hbm, wk_ref), (wv_hbm, wv_ref), (wq_hbm, wq_ref)))
    ]
    for load in loads:
        load.start()
    right, left, across = shifted(x=1), shifted(x=-1), shifted(z=1)
    up, down, mate = shifted(y=1), shifted(y=-1), shifted(other_core=True)
    rows_of = [shifted(row=d) for d in (1, 2, 3)]
    greet([right, left, across, up, down, mate] + rows_of)
    tok, key = (token_send, token_recv), (key_send, key_recv)
    sent = []
    half = ROWS // 2

    def token_rows(c, part=None):
        if part is None:
            return pl.ds(c * ROWS, ROWS)
        return pl.ds(c * ROWS + part * half, half)

    def source_of(dz, c):
        if dz == 0:
            return tokens_ref.at[token_rows(c)]
        return held.at[1, 0, token_rows(c)]

    def across_send(c):
        copy = send(
            tokens_ref.at[token_rows(c)], held.at[1, 0, token_rows(c)], tok, c * 9 + 8, across
        )
        sent.append(copy)
        return copy

    def side_sends(c, dz):
        source = source_of(dz, c)
        a = send(source, held.at[dz, 3, token_rows(c)], tok, c * 9 + dz * 4, right)
        b = send(source, held.at[dz, 1, token_rows(c)], tok, c * 9 + dz * 4 + 1, left)
        sent.extend((a, b))
        return a, b

    def side_forwards(c, dz):
        rows = token_rows(c, 0)
        a = send(held.at[dz, 3, rows], held.at[dz, 2, rows], tok, c * 9 + dz * 4 + 2, right)
        rows = token_rows(c, 1)
        b = send(held.at[dz, 1, rows], held.at[dz, 2, rows], tok, c * 9 + dz * 4 + 3, left)
        sent.extend((a, b))
        return a, b

    def weights_at(dz, dx):
        owner = lax.rem(zhi + dz, 2) * 4 + lax.rem(x + dx, 4)
        rows = pl.ds(pl.multiple_of(owner * 512, 512), 512)
        return jnp.concatenate([wk_ref[rows, :], wv_ref[rows, :], wq_ref[rows, :]], axis=1)

    def product(c, dz, dx):
        if dz == 0 and dx == 0:
            features = tokens_ref[token_rows(c), :]
        else:
            features = held[dz, dx, token_rows(c), :]
        return jnp.dot(features, weights_at(dz, dx), preferred_element_type=jnp.float32)

    def group(c, g, b):
        return kv_ref.at[c, g, b]

    def key_rows(c):
        out = []
        for i, peer in enumerate(rows_of):
            block = kv_ref.at[c, core, y, row]
            out.append(send(block, block, key, c * 11 + i, peer))
        sent.extend(out)
        return out

    def key_sides(c, arrivals):
        for copy in arrivals:
            copy.wait_recv()
        mine = group(c, core, y)
        a = send(mine, mine, key, c * 11 + 3, up)
        b = send(mine, mine, key, c * 11 + 4, down)
        m = send(mine, mine, key, c * 11 + 7, mate)
        sent.extend((a, b, m))
        return a, b, m

    def key_forwards(c, sides):
        a, b, m = sides
        a.wait_recv()
        behind = lax.rem(y + 3, 4)
        part = kv_ref.at[c, core, behind, pl.ds(0, 2)]
        fa = send(part, part, key, c * 11 + 5, up)
        got = group(c, core, behind)
        ma = send(got, got, key, c * 11 + 8, mate)
        b.wait_recv()
        ahead = lax.rem(y + 1, 4)
        part = kv_ref.at[c, core, ahead, pl.ds(2, 2)]
        fb = send(part, part, key, c * 11 + 6, down)
        got = group(c, core, ahead)
        mb = send(got, got, key, c * 11 + 9, mate)
        sent.extend((fa, fb, ma, mb))
        return fa, fb, m, ma, mb

    def key_last(c, moved):
        fa, fb, m, ma, mb = moved
        fa.wait_recv()
        fb.wait_recv()
        got = group(c, core, lax.rem(y + 2, 4))
        mc = send(got, got, key, c * 11 + 10, mate)
        sent.append(mc)
        return m, ma, mb, mc

    across_of, own_of, far_of, rows_at, sides_at, moved_at, mates = {}, {}, {}, {}, {}, {}, []
    for c in range(2):
        across_of[c] = across_send(c)
        own_of[c] = side_sends(c, 0)
    across_of[0].wait_recv()
    far_of[0] = side_sends(0, 1)
    for c in range(CHUNKS):
        for copy in own_of[c]:
            copy.wait_recv()
        near = side_forwards(c, 0)
        if c + 2 < CHUNKS:
            across_of[c + 2] = across_send(c + 2)
        if c >= 1:
            sides_at[c - 1] = key_sides(c - 1, rows_at[c - 1])
        for copy in far_of[c]:
            copy.wait_recv()
        far = side_forwards(c, 1)
        if c + 2 < CHUNKS:
            own_of[c + 2] = side_sends(c + 2, 0)
        if c + 1 < CHUNKS:
            across_of[c + 1].wait_recv()
            far_of[c + 1] = side_sends(c + 1, 1)
        if c == 0:
            for load in loads:
                load.wait()
        total = product(c, 0, 0)
        for dz, dx in ((0, 3), (0, 1), (1, 0), (1, 3), (1, 1)):
            total = total + product(c, dz, dx)
        for copy in near:
            copy.wait_recv()
        total = total + product(c, 0, 2)
        for copy in far:
            copy.wait_recv()
        total = total + product(c, 1, 2)
        cosine, sine = cos_ref[token_rows(c), :], sin_ref[token_rows(c), :]

        def turned(vectors):
            return (vectors * cosine + pltpu.roll(vectors, HD // 2, 1) * sine).astype(jnp.bfloat16)

        kv_ref[c, core, y, row, :ROWS, :] = turned(total[:, :HD])
        kv_ref[c, core, y, row, ROWS:TAG, :] = total[:, HD : 2 * HD].astype(jnp.bfloat16)
        tag = ids_ref[0, c // 2].astype(jnp.float32)
        kv_ref[c, core, y, row, TAG:, :] = jnp.full((16, HD), tag, jnp.float32).astype(jnp.bfloat16)
        for head in range(4):
            at = head * SPAN + (c % 2) * ROWS
            q_ref[c // 2, at : at + ROWS, :] = turned(total[:, (2 + head) * HD : (3 + head) * HD])
        rows_at[c] = key_rows(c)
        if c >= 1:
            moved_at[c - 1] = key_forwards(c - 1, sides_at[c - 1])
        if c >= 2:
            mates.extend(key_last(c - 2, moved_at[c - 2]))
    last = CHUNKS - 1
    mates.extend(key_last(last - 1, moved_at[last - 1]))
    sides_at[last] = key_sides(last, rows_at[last])
    moved_at[last] = key_forwards(last, sides_at[last])
    mates.extend(key_last(last, moved_at[last]))
    for copy in mates:
        copy.wait_recv()
    for copy in sent:
        copy.wait_send()


def project(span_ids, tokens, q_weight, k_weight, v_weight, cosine, sine):
    vmem = pl.BlockSpec(memory_space=pltpu.VMEM)
    hbm = pl.BlockSpec(memory_space=pl.ANY)
    return pl.pallas_call(
        project_kernel,
        out_shape=(
            jax.ShapeDtypeStruct((2, 4 * SPAN, HD), jnp.bfloat16),
            jax.ShapeDtypeStruct((CHUNKS, 2, 4, 4, BLOCK, HD), jnp.bfloat16),
        ),
        in_specs=[pl.BlockSpec(memory_space=pltpu.SMEM), vmem, hbm, hbm, hbm, vmem, vmem],
        out_specs=(vmem, vmem),
        scratch_shapes=[
            pltpu.VMEM(q_weight.shape, jnp.bfloat16),
            pltpu.VMEM(k_weight.shape, jnp.bfloat16),
            pltpu.VMEM(v_weight.shape, jnp.bfloat16),
            pltpu.VMEM((2, 4) + tokens.shape, jnp.bfloat16),
            pltpu.SemaphoreType.DMA((3,)),
            pltpu.SemaphoreType.DMA((CHUNKS * 9,)),
            pltpu.SemaphoreType.DMA((CHUNKS * 9,)),
            pltpu.SemaphoreType.DMA((CHUNKS * 11,)),
            pltpu.SemaphoreType.DMA((CHUNKS * 11,)),
        ],
        compiler_params=pltpu.CompilerParams(
            collective_id=0, has_side_effects=True, vmem_limit_bytes=40 * 1024 * 1024
        ),
        name="project",
    )(span_ids, tokens, q_weight, k_weight, v_weight, cosine, sine)


def attend_kernel(info, q_ref, kv_ref, start_ref, out_ref, top_ref, acc_ref):
    heads = q_ref.shape[1] // SPAN
    scale = LOG2E * HD**-0.5
    ones = jnp.ones((SPAN, HD), jnp.bfloat16)

    def block(half, span, masked, first):
        place = info[span]
        first_place = (place // 32) * 64 + place % 32
        places = (first_place, first_place + 32)
        keys = jnp.concatenate([kv_ref[at, :ROWS, :] for at in places], axis=0)
        values = jnp.concatenate([kv_ref[at, ROWS:TAG, :] for at in places], axis=0)
        values = jnp.concatenate([values, ones], axis=1)
        if masked:
            key = span * SPAN + lax.broadcasted_iota(jnp.int32, (SPAN, SPAN), 1)
            start = start_ref[half]
            seen = key >= jnp.concatenate([start, start], axis=1)
            if first:
                query = span * SPAN + lax.broadcasted_iota(jnp.int32, (SPAN, SPAN), 0)
                seen = seen & (key <= query)
        for head in range(heads):
            rows = slice(head * SPAN, (head + 1) * SPAN)
            score = lax.dot_general(
                q_ref[half, rows, :],
                keys,
                (((1,), (1,)), ((), ())),
                preferred_element_type=jnp.float32,
            )
            score = score * scale
            if masked:
                score = jnp.where(seen, score, floor_score)
            top = jnp.max(score, axis=1, keepdims=True)
            if first:
                weight = jnp.exp2(score - top)
                top_ref[rows, :] = jnp.broadcast_to(top, (SPAN, HD))
            else:
                before = top_ref[rows, :]
                now = jnp.maximum(before, top)
                weight = jnp.exp2(score - jnp.concatenate([now, now], axis=1))
                fade = jnp.exp2(before - now)
                top_ref[rows, :] = now
            mixed = jnp.dot(
                weight.astype(jnp.bfloat16), values, preferred_element_type=jnp.float32
            )
            if not first:
                mixed = mixed + acc_ref[rows, :] * jnp.concatenate([fade, fade], axis=1)
            acc_ref[rows, :] = mixed

    for half in range(2):
        own, low, clear = info[64 + half], info[66 + half], info[68 + half]
        block(half, own, True, True)
        lax.fori_loop(low, clear, lambda s, c: (block(half, s, True, False), c)[1], 0)
        lax.fori_loop(clear, own, lambda s, c: (block(half, s, False, False), c)[1], 0)
        for head in range(heads):
            rows = slice(head * SPAN, (head + 1) * SPAN)
            mixed = acc_ref[rows, :HD] / acc_ref[rows, HD:]
            out_ref[half * SPAN : (half + 1) * SPAN, head * HD : (head + 1) * HD] = mixed.astype(
                jnp.bfloat16
            )


def attend(info, queries, gathered, starts):
    vmem = pl.BlockSpec(memory_space=pltpu.VMEM)
    rows = queries.shape[1]
    heads = rows // SPAN
    return pl.pallas_call(
        attend_kernel,
        out_shape=jax.ShapeDtypeStruct((2 * SPAN, heads * HD), jnp.bfloat16),
        in_specs=[pl.BlockSpec(memory_space=pltpu.SMEM), vmem, vmem, vmem],
        out_specs=vmem,
        scratch_shapes=[
            pltpu.VMEM((rows, HD), jnp.float32),
            pltpu.VMEM((rows, 2 * HD), jnp.float32),
        ],
        compiler_params=pltpu.CompilerParams(vmem_limit_bytes=32 * 1024 * 1024),
        name="attend",
    )(info, queries, gathered, starts)


def combine_kernel(
    attn_ref, weight_ref, out_ref, far_out, far_in, near_out, near_in, over_out, over_in, kept,
    send_sem, recv_sem,
):
    x, zhi = lax.axis_index("tp_1"), lax.axis_index("tp_0")
    right, left, across = shifted(x=1), shifted(x=-1), shifted(z=1)
    greet([right, left, across])
    sems = (send_sem, recv_sem)
    steps = kept.shape[0]
    size = kept.shape[1]
    half = size // 2
    width = out_ref.shape[1]
    sent = []

    def share(c, dx):
        rows = attn_ref[c * size : (c + 1) * size, :]
        terms = []
        for dz in range(2):
            owner = lax.rem(zhi + dz, 2) * 4 + lax.rem(x + dx, 4)
            columns = pl.ds(pl.multiple_of(owner * width, width), width)
            terms.append(
                jnp.dot(rows, weight_ref[:, columns], preferred_element_type=jnp.float32)
            )
        return jnp.concatenate(terms, axis=1)

    def open_step(c):
        far = share(c, 2).astype(jnp.bfloat16)
        far_out[c, 0] = far[:half]
        far_out[c, 1] = far[half:]
        a = send(far_out.at[c, 0], far_in.at[c, 0], sems, c * 7, right)
        b = send(far_out.at[c, 1], far_in.at[c, 1], sems, c * 7 + 1, left)
        to_right, to_left = share(c, 1), share(c, 3)
        near_out[c, 0, 1] = to_right[half:].astype(jnp.bfloat16)
        d = send(near_out.at[c, 0, 1], near_in.at[c, 0, 1], sems, c * 7 + 2, right)
        near_out[c, 1, 0] = to_left[:half].astype(jnp.bfloat16)
        e = send(near_out.at[c, 1, 0], near_in.at[c, 1, 0], sems, c * 7 + 3, left)
        near_out[c, 0, 0] = to_right[:half].astype(jnp.bfloat16)
        near_out[c, 1, 1] = to_left[half:].astype(jnp.bfloat16)
        sent.extend((a, b, d, e))
        return a, b, d, e

    def pass_on(c, opened):
        a, b, d, e = opened
        a.wait_recv()
        near_out[c, 0, 0] = (
            near_out[c, 0, 0].astype(jnp.float32) + far_in[c, 0].astype(jnp.float32)
        ).astype(jnp.bfloat16)
        f = send(near_out.at[c, 0, 0], near_in.at[c, 0, 0], sems, c * 7 + 4, right)
        b.wait_recv()
        near_out[c, 1, 1] = (
            near_out[c, 1, 1].astype(jnp.float32) + far_in[c, 1].astype(jnp.float32)
        ).astype(jnp.bfloat16)
        g = send(near_out.at[c, 1, 1], near_in.at[c, 1, 1], sems, c * 7 + 5, left)
        sent.extend((f, g))
        return d, e, f, g

    def cross(c, passed):
        total = share(c, 0)
        for copy in passed:
            copy.wait_recv()
        for side in range(2):
            both = jnp.concatenate([near_in[c, side, 0], near_in[c, side, 1]], axis=0)
            total = total + both.astype(jnp.float32)
        over_out[c] = total[:, width:].astype(jnp.bfloat16)
        kept[c] = total[:, :width]
        copy = send(over_out.at[c], over_in.at[c], sems, c * 7 + 6, across)
        sent.append(copy)
        return copy

    def close(c, crossed):
        crossed.wait_recv()
        out_ref[c * size : (c + 1) * size, :] = (
            kept[c] + over_in[c].astype(jnp.float32)
        ).astype(jnp.bfloat16)

    opened, passed, crossed = {}, {}, {}
    for c in range(2):
        opened[c] = open_step(c)
    for c in range(steps):
        passed[c] = pass_on(c, opened[c])
        if c + 2 < steps:
            opened[c + 2] = open_step(c + 2)
        if c >= 1:
            crossed[c - 1] = cross(c - 1, passed[c - 1])
        if c >= 2:
            close(c - 2, crossed[c - 2])
    crossed[steps - 1] = cross(steps - 1, passed[steps - 1])
    close(steps - 2, crossed[steps - 2])
    close(steps - 1, crossed[steps - 1])
    for copy in sent:
        copy.wait_send()


STEPS = 4


def combine(attention, o_weight):
    vmem = pl.BlockSpec(memory_space=pltpu.VMEM)
    rows, width = attention.shape[0], o_weight.shape[1] // 8
    size = rows // STEPS
    half = (size // 2, 2 * width)
    return pl.pallas_call(
        combine_kernel,
        out_shape=jax.ShapeDtypeStruct((rows, width), jnp.bfloat16),
        in_specs=[vmem, vmem],
        out_specs=vmem,
        scratch_shapes=[
            pltpu.VMEM((STEPS, 2) + half, jnp.bfloat16),
            pltpu.VMEM((STEPS, 2) + half, jnp.bfloat16),
            pltpu.VMEM((STEPS, 2, 2) + half, jnp.bfloat16),
            pltpu.VMEM((STEPS, 2, 2) + half, jnp.bfloat16),
            pltpu.VMEM((STEPS, size, width), jnp.bfloat16),
            pltpu.VMEM((STEPS, size, width), jnp.bfloat16),
            pltpu.VMEM((STEPS, size, width), jnp.float32),
            pltpu.SemaphoreType.DMA((STEPS * 7,)),
            pltpu.SemaphoreType.DMA((STEPS * 7,)),
        ],
        compiler_params=pltpu.CompilerParams(
            collective_id=1, has_side_effects=True, vmem_limit_bytes=32 * 1024 * 1024
        ),
        name="combine",
    )(attention, o_weight)


def plan(span_table, own, starts):
    blocks = jnp.arange(64, dtype=jnp.int32)
    where = jnp.sum(
        jnp.where(span_table.reshape(1, 64) == blocks[:, None], blocks[None, :], 0), axis=1
    )
    low = starts[:, 0] // SPAN
    clear = jnp.minimum((starts[:, -1] + SPAN - 1) // SPAN, own)
    return jnp.concatenate([where, own, low, clear, jnp.zeros(58, jnp.int32)])


def turn_tables(positions):
    half_size = HD // 2
    exponent = jnp.arange(half_size, dtype=jnp.float32) * (2.0 / HD)
    inverse_freq = theta_base ** (-exponent)
    angles = positions.astype(jnp.float32)[:, None] * inverse_freq[None, :]
    cosine, sine = jnp.cos(angles), jnp.sin(angles)
    return jnp.concatenate([cosine, cosine], axis=1), jnp.concatenate([-sine, sine], axis=1)


def per_device(tokens, span_ids, positions, q_weight, k_weight, v_weight, o_weight):
    cosine, sine = turn_tables(positions)
    queries, held = project(span_ids, tokens, q_weight, k_weight, v_weight, cosine, sine)
    span_table = held[::2, :, :, :, TAG, 0].astype(jnp.int32)
    own = span_ids.reshape(2)
    offsets = jnp.arange(SPAN, dtype=jnp.int32)
    starts = own[:, None] * SPAN + offsets[None, :] - positions.reshape(2, SPAN)
    info = plan(span_table, own, starts)
    starts = jnp.broadcast_to(starts[:, :, None], (2, SPAN, HD))
    attention = attend(info, queries, held.reshape(-1, BLOCK, HD), starts)
    return combine(attention, o_weight)


def solution(mesh):
    split = Mesh(mesh.devices.reshape(4, 4, 2, 2, 4), ("cp_0", "cp_1", "cp_2", "tp_0", "tp_1"))
    placed = (P(CP, TP), P(CP, None), P(CP), P(None, TP), P(None, TP), P(None, TP), P(TP, None))
    return jax.shard_map(
        per_device, mesh=split, in_specs=placed, out_specs=P(CP, TP), check_vma=False
    )
```

```python
import jax
import jax.numpy as jnp
from jax import lax
from jax.experimental import pallas as pl
from jax.experimental.pallas import tpu as pltpu
from jax.sharding import Mesh
from jax.sharding import PartitionSpec as P

HD = 128
SPAN = 256
LOG2E = 1.4426950408889634
TP = ("tp_0", "tp_1")
CP = ("cp_0", "cp_1", "cp_2")


theta_base = 500000.0
floor_score = -1e30


MESH = pl.DeviceIdType.MESH
CHUNKS = 4
ROWS = 128
TAG = 2 * ROWS
BLOCK = TAG + 16


def shifted(x=0, y=0, z=0, row=0, other_core=False):
    place = {}
    if x:
        place["tp_1"] = lax.rem(lax.axis_index("tp_1") + x + 4, 4)
    if y:
        place["cp_1"] = lax.rem(lax.axis_index("cp_1") + y + 4, 4)
    if z:
        place["tp_0"] = 1 - lax.axis_index("tp_0")
    if row:
        place["cp_0"] = lax.rem(lax.axis_index("cp_0") + row + 4, 4)
    if other_core:
        place["cp_2"] = 1 - lax.axis_index("cp_2")
    return place


def greet(peers):
    barrier = pltpu.get_barrier_semaphore()
    for peer in peers:
        pl.semaphore_signal(barrier, inc=1, device_id=peer, device_id_type=MESH)
    pl.semaphore_wait(barrier, len(peers))


def sending(source, target, sems, index, peer, arrival=None):
    return pltpu.make_async_remote_copy(
        src_ref=source,
        dst_ref=target,
        send_sem=sems[0].at[index],
        recv_sem=sems[1].at[index if arrival is None else arrival],
        device_id=peer,
        device_id_type=MESH,
    )


def send(source, target, sems, index, peer):
    copy = sending(source, target, sems, index, peer)
    copy.start()
    return copy


def columns_of(line):
    return jnp.broadcast_to(line, (128, 128)).T


def turn_table(line):
    lane = lax.rem(lax.broadcasted_iota(jnp.int32, (8, 128), 1), HD // 2)
    frequency = jnp.zeros((8, 128), jnp.float32)
    for j in range(HD // 2):
        frequency = jnp.where(lane == j, theta_base ** (-2.0 * j / HD), frequency)
    angle = columns_of(line.astype(jnp.float32)) * frequency[:1]
    turns = jnp.floor(angle * 0.6366197723675814 + 0.5)
    rest = ((angle - turns * 1.5703125) - turns * 4.837512969970703e-4) - turns * 7.549789954891882e-8
    square = rest * rest
    cosine = (2.443315711809948e-5 * square - 1.388731625493765e-3) * square + 4.166664568298827e-2
    cosine = cosine * square * square - 0.5 * square + 1.0
    sine = (-1.9515295891e-4 * square + 8.3321608736e-3) * square - 1.6666654611e-1
    sine = sine * square * rest + rest
    quarter = turns - 4.0 * jnp.floor(turns * 0.25)
    odd = (quarter == 1.0) | (quarter == 3.0)
    cos_all = jnp.where(odd, sine, cosine)
    sin_all = jnp.where(odd, cosine, sine)
    cos_all = jnp.where((quarter == 1.0) | (quarter == 2.0), -cos_all, cos_all)
    sin_all = jnp.where(quarter >= 2.0, -sin_all, sin_all)
    side = lax.broadcasted_iota(jnp.int32, (128, 128), 1)
    return cos_all, jnp.where(side < HD // 2, -sin_all, sin_all)


ORDER = (
    "n0", "a0", "n1", "f0", "a1", "d0", "x0", "n2", "f1", "n3",
    "a2", "d1", "x1", "s0", "f2", "a3", "d2", "x2", "s1", "w0",
    "f3", "d3", "l0", "x3", "s2", "w1", "s3", "w2", "l1", "w3",
    "l2", "l3",
)
TOKEN_SEMS = 9
KEY_SEMS = 20


def project_kernel(
    ids_hbm,
    positions_hbm,
    tokens_hbm,
    wq_hbm,
    wk_hbm,
    wv_hbm,
    q_ref,
    kv_ref,
    ids_ref,
    positions_ref,
    tokens_ref,
    wq_ref,
    wk_ref,
    wv_ref,
    held,
    load_sem,
    token_send,
    token_recv,
    key_send,
    key_recv,
):
    x, zhi = lax.axis_index("tp_1"), lax.axis_index("tp_0")
    row, y, core = lax.axis_index("cp_0"), lax.axis_index("cp_1"), lax.axis_index("cp_2")
    loads = [
        pltpu.make_async_copy(a, b, load_sem.at[i])
        for i, (a, b) in enumerate(
            (
                (tokens_hbm, tokens_ref),
                (ids_hbm, ids_ref),
                (positions_hbm, positions_ref),
                (wk_hbm, wk_ref),
                (wv_hbm, wv_ref),
                (wq_hbm, wq_ref),
            )
        )
    ]
    for load in loads:
        load.start()
    right, left, across = shifted(x=1), shifted(x=-1), shifted(z=1)
    up, down, mate = shifted(y=1), shifted(y=-1), shifted(other_core=True)
    rows_of = [shifted(row=d) for d in (1, 2, 3)]
    greet([right, left, across, up, down, mate] + rows_of)
    tok, key = (token_send, token_recv), (key_send, key_recv)
    sent = []
    half = ROWS // 2
    inner = (row == 1) | (row == 2)
    loads[0].wait()

    def token_rows(c, part=None):
        if part is None:
            return pl.ds(c * ROWS, ROWS)
        return pl.ds(c * ROWS + part * half, half)

    def across_send(c):
        rows = token_rows(c)
        copy = send(
            tokens_ref.at[rows], held.at[1, 0, rows], tok, c * TOKEN_SEMS + 8, across
        )
        sent.append(copy)
        return copy

    def side_sends(c, dz):
        rows = token_rows(c)
        source = held.at[1, 0, rows] if dz else tokens_ref.at[rows]
        a = send(source, held.at[dz, 3, rows], tok, c * TOKEN_SEMS + dz * 4, right)
        b = send(source, held.at[dz, 1, rows], tok, c * TOKEN_SEMS + dz * 4 + 1, left)
        sent.extend((a, b))
        return a, b

    def side_forwards(c, dz):
        at = c * TOKEN_SEMS + dz * 4
        rows = token_rows(c, 0)
        a = send(held.at[dz, 3, rows], held.at[dz, 2, rows], tok, at + 2, right)
        rows = token_rows(c, 1)
        b = send(held.at[dz, 1, rows], held.at[dz, 2, rows], tok, at + 3, left)
        sent.extend((a, b))
        return a, b

    def product(c, dz, dx):
        owner = lax.rem(zhi + dz, 2) * 4 + lax.rem(x + dx, 4)
        rows = pl.ds(pl.multiple_of(owner * 512, 512), 512)
        weights = jnp.concatenate([wk_ref[rows, :], wv_ref[rows, :], wq_ref[rows, :]], axis=1)
        if dz == 0 and dx == 0:
            features = tokens_ref[token_rows(c), :]
        else:
            features = held[dz, dx, token_rows(c), :]
        return jnp.dot(features, weights, preferred_element_type=jnp.float32)

    def key_rows(c):
        at = c * KEY_SEMS
        block = kv_ref.at[c, core, y, row]
        out = []
        for d, skip in ((1, row == 3), (2, None), (3, row == 0)):
            copy = sending(block, block, key, at + d - 1, rows_of[d - 1])
            if skip is None:
                copy.start()
            else:
                pl.when(jnp.logical_not(skip))(copy.start)
            out.append(copy)
        return out, [key_side(c, 0)]

    def key_side(c, d):
        block = kv_ref.at[c, core, y, lax.rem(row + 4 - d, 4)]
        a = send(block, block, key, c * KEY_SEMS + 4 + d, up)
        b = send(block, block, key, c * KEY_SEMS + 8 + d, down)
        sent.extend((a, b))
        return a, b

    def key_relay(c):
        at = c * KEY_SEMS
        block = kv_ref.at[c, core, y, lax.rem(row + 2, 4)]
        end = {"cp_0": jnp.where(row == 2, 3, 0)}
        arrival = at + jnp.where(row == 2, 2, 0)
        return sending(block, block, key, at + 3, end, arrival)

    def key_sides(c, started):
        out, sides = started
        relay = key_relay(c)
        out[1].wait_recv()
        pl.when(inner)(relay.start)
        sides.append(key_side(c, 2))
        out[0].wait_recv()
        sides.append(key_side(c, 1))
        out[2].wait_recv()
        sides.append(key_side(c, 3))
        mine = kv_ref.at[c, core, y]
        m = send(mine, mine, key, c * KEY_SEMS + 16, mate)
        sent.append(m)
        return sides, m, relay

    def key_forwards(c, state):
        sides, m, relay = state
        at = c * KEY_SEMS
        behind, ahead = lax.rem(y + 3, 4), lax.rem(y + 1, 4)
        forwards = []
        for place, d in enumerate((0, 2, 1, 3)):
            a, b = sides[place]
            block_at = lax.rem(row + 4 - d, 4)
            a.wait_recv()
            b.wait_recv()
            if d in (0, 1):
                block = kv_ref.at[c, core, behind, block_at]
                f = send(block, block, key, at + 12 + d, up)
            else:
                block = kv_ref.at[c, core, ahead, block_at]
                f = send(block, block, key, at + 12 + d, down)
            forwards.append(f)
        mates = [m]
        for i, at_y in enumerate((behind, ahead)):
            got = kv_ref.at[c, core, at_y]
            mates.append(send(got, got, key, at + 17 + i, mate))
        sent.extend(forwards + mates[1:])
        return forwards, mates

    def key_last(c, moved):
        forwards, mates = moved
        for f in forwards:
            f.wait_recv()
        got = kv_ref.at[c, core, lax.rem(y + 2, 4)]
        mc = send(got, got, key, c * KEY_SEMS + 19, mate)
        sent.append(mc)
        return mates + [mc]

    across_of, own_of, far_of, near_on, far_on = {}, {}, {}, {}, {}
    rows_at, sides_at, moved_at, totals, mates = {}, {}, {}, {}, []

    def near_step(c):
        for copy in own_of[c]:
            copy.wait_recv()
        near_on[c] = side_forwards(c, 0)

    def across_step(c):
        if c < CHUNKS:
            across_of[c].wait_recv()
            far_of[c] = side_sends(c, 1)

    def far_step(c):
        if c < CHUNKS:
            for copy in far_of[c]:
                copy.wait_recv()
            far_on[c] = side_forwards(c, 1)

    def multiply(c):
        total = product(c, 0, 0)
        for dz, dx in ((0, 3), (0, 1), (1, 0), (1, 3), (1, 1)):
            total = total + product(c, dz, dx)
        totals[c] = total

    def finish(c):
        total = totals[c]
        cosine, sine = turn_table(positions_ref[c : c + 1, :])
        for copy in near_on[c]:
            copy.wait_recv()
        total = total + product(c, 0, 2)
        for copy in far_on[c]:
            copy.wait_recv()
        total = total + product(c, 1, 2)

        def turned(vectors):
            return (vectors * cosine + pltpu.roll(vectors, HD // 2, 1) * sine).astype(jnp.bfloat16)

        kv_ref[c, core, y, row, :ROWS, :] = turned(total[:, :HD])
        kv_ref[c, core, y, row, ROWS:TAG, :] = total[:, HD : 2 * HD].astype(jnp.bfloat16)
        tag = ids_ref[0, c // 2].astype(jnp.float32)
        kv_ref[c, core, y, row, TAG:, :] = jnp.full((16, HD), tag, jnp.float32).astype(jnp.bfloat16)
        rows_at[c] = key_rows(c)
        for head in range(4):
            at = head * SPAN + (c % 2) * ROWS
            q_ref[c // 2, at : at + ROWS, :] = turned(total[:, (2 + head) * HD : (3 + head) * HD])

    def side_step(c):
        sides_at[c] = key_sides(c, rows_at[c])

    def forward_step(c):
        moved_at[c] = key_forwards(c, sides_at[c])

    def last_step(c):
        mates.extend(key_last(c, moved_at[c]))

    for c in range(CHUNKS):
        own_of[c] = side_sends(c, 0)
        across_of[c] = across_send(c)
    actions = {
        "n": near_step,
        "a": across_step,
        "f": far_step,
        "d": multiply,
        "x": finish,
        "s": side_step,
        "w": forward_step,
        "l": last_step,
    }
    for action in ORDER:
        if action == "d0":
            for load in loads[1:]:
                load.wait()
        actions[action[0]](int(action[1:]))
    for copy in mates:
        copy.wait_recv()
    for copy in sent:
        copy.wait_send()
    for c in range(CHUNKS):
        out = rows_at[c][0]
        out[1].wait_send()
        pl.when(row != 3)(out[0].wait_send)
        pl.when(row != 0)(out[2].wait_send)
        pl.when(inner)(sides_at[c][2].wait_send)


def project(span_ids, positions, tokens, q_weight, k_weight, v_weight):
    vmem = pl.BlockSpec(memory_space=pltpu.VMEM)
    hbm = pl.BlockSpec(memory_space=pltpu.HBM)
    return pl.pallas_call(
        project_kernel,
        out_shape=(
            jax.ShapeDtypeStruct((2, 4 * SPAN, HD), jnp.bfloat16),
            jax.ShapeDtypeStruct((CHUNKS, 2, 4, 4, BLOCK, HD), jnp.bfloat16),
        ),
        in_specs=[hbm] * 6,
        out_specs=(vmem, vmem),
        scratch_shapes=[
            pltpu.SMEM(span_ids.shape, jnp.int32),
            pltpu.VMEM(positions.shape, jnp.int32),
            pltpu.VMEM(tokens.shape, jnp.bfloat16),
            pltpu.VMEM(q_weight.shape, jnp.bfloat16),
            pltpu.VMEM(k_weight.shape, jnp.bfloat16),
            pltpu.VMEM(v_weight.shape, jnp.bfloat16),
            pltpu.VMEM((2, 4) + tokens.shape, jnp.bfloat16),
            pltpu.SemaphoreType.DMA((6,)),
            pltpu.SemaphoreType.DMA((CHUNKS * TOKEN_SEMS,)),
            pltpu.SemaphoreType.DMA((CHUNKS * TOKEN_SEMS,)),
            pltpu.SemaphoreType.DMA((CHUNKS * KEY_SEMS,)),
            pltpu.SemaphoreType.DMA((CHUNKS * KEY_SEMS,)),
        ],
        compiler_params=pltpu.CompilerParams(
            collective_id=0, has_side_effects=True, vmem_limit_bytes=26 * 1024 * 1024
        ),
        name="project",
    )(
        *(
            pltpu.with_memory_space_constraint(array, pltpu.HBM)
            for array in (span_ids, positions, tokens, q_weight, k_weight, v_weight)
        )
    )


def attend_kernel(
    ids_hbm, positions_hbm, q_ref, kv_ref, out_ref, ids, places_of, positions_ref, top_ref, acc_ref,
    start_ref, table_ref, where, sems,
):
    loads = [
        pltpu.make_async_copy(a, b, sems.at[i + 1])
        for i, (a, b) in enumerate(
            ((ids_hbm, ids), (positions_hbm, positions_ref), (positions_hbm, places_of))
        )
    ]
    for load in loads:
        load.start()
    heads = q_ref.shape[1] // SPAN
    scale = LOG2E * HD**-0.5
    ones = jnp.ones((SPAN, HD), jnp.bfloat16)
    lane = lax.broadcasted_iota(jnp.int32, (8, 128), 1).astype(jnp.float32)
    table = jnp.zeros((8, 128), jnp.int32)
    for block in range(64):
        at = (block // 32) * 64 + block % 32
        tag = kv_ref[at, TAG:, :].astype(jnp.float32)[:8]
        table = table + jnp.where(tag == lane, block, 0)
    table_ref[...] = table
    fetch = pltpu.make_async_copy(table_ref, where, sems.at[0])
    fetch.start()
    row, y, core = lax.axis_index("cp_0"), lax.axis_index("cp_1"), lax.axis_index("cp_2")
    home = core * 16 + y * 4 + row
    for load in loads:
        load.wait()
    for half in range(2):
        own = ids[0, half]
        for part in range(2):
            line = 2 * half + part
            column = columns_of(positions_ref[line : line + 1, :].astype(jnp.float32))
            place = own * SPAN + part * 128
            place = place + lax.broadcasted_iota(jnp.int32, (128, 128), 0)
            start_ref[half, part * 128 : (part + 1) * 128, :] = place - column.astype(jnp.int32)

    def block(half, span, place, masked, first):
        first_place = (place // 32) * 64 + lax.rem(place, 32)
        places = (first_place, first_place + 32)
        keys = jnp.concatenate([kv_ref[at, :ROWS, :] for at in places], axis=0)
        values = jnp.concatenate([kv_ref[at, ROWS:TAG, :] for at in places], axis=0)
        values = jnp.concatenate([values, ones], axis=1)
        if masked:
            key = span * SPAN + lax.broadcasted_iota(jnp.int32, (SPAN, SPAN), 1)
            start = start_ref[half]
            seen = key >= jnp.concatenate([start, start], axis=1)
            if first:
                query = span * SPAN + lax.broadcasted_iota(jnp.int32, (SPAN, SPAN), 0)
                seen = seen & (key <= query)
        for head in range(heads):
            rows = slice(head * SPAN, (head + 1) * SPAN)
            score = lax.dot_general(
                q_ref[half, rows, :],
                keys,
                (((1,), (1,)), ((), ())),
                preferred_element_type=jnp.float32,
            )
            score = score * scale
            if masked:
                score = jnp.where(seen, score, floor_score)
            top = jnp.max(score, axis=1, keepdims=True)
            if first:
                weight = jnp.exp2(score - top)
                top_ref[half, rows, :] = jnp.broadcast_to(top, (SPAN, HD))
            else:
                before = top_ref[half, rows, :]
                now = jnp.maximum(before, top)
                weight = jnp.exp2(score - jnp.concatenate([now, now], axis=1))
                fade = jnp.exp2(before - now)
                top_ref[half, rows, :] = now
            mixed = jnp.dot(
                weight.astype(jnp.bfloat16), values, preferred_element_type=jnp.float32
            )
            if not first:
                mixed = mixed + acc_ref[half, rows, :] * jnp.concatenate([fade, fade], axis=1)
            acc_ref[half, rows, :] = mixed

    for half in range(2):
        block(half, ids[0, half], home + 32 * half, True, True)
    fetch.wait()
    for half in range(2):
        own = ids[0, half]
        low = (own * SPAN - places_of[2 * half, 0]) // SPAN
        clear = (own * SPAN + 2 * SPAN - 2 - places_of[2 * half + 1, 127]) // SPAN
        clear = jnp.minimum(clear, own)

        def masked_step(span, carry):
            block(half, span, where[0, span], True, False)
            return carry

        def clear_step(span, carry):
            block(half, span, where[0, span], False, False)
            return carry

        lax.fori_loop(low, clear, masked_step, 0)
        lax.fori_loop(clear, own, clear_step, 0)
        for head in range(heads):
            rows = slice(head * SPAN, (head + 1) * SPAN)
            mixed = acc_ref[half, rows, :HD] / acc_ref[half, rows, HD:]
            out_ref[half * SPAN : (half + 1) * SPAN, head * HD : (head + 1) * HD] = mixed.astype(
                jnp.bfloat16
            )


def attend(span_ids, positions, queries, held):
    vmem = pl.BlockSpec(memory_space=pltpu.VMEM)
    hbm = pl.BlockSpec(memory_space=pltpu.HBM)
    rows = queries.shape[1]
    heads = rows // SPAN
    return pl.pallas_call(
        attend_kernel,
        out_shape=jax.ShapeDtypeStruct((2 * SPAN, heads * HD), jnp.bfloat16),
        in_specs=[hbm, hbm, vmem, vmem],
        out_specs=vmem,
        scratch_shapes=[
            pltpu.SMEM(span_ids.shape, jnp.int32),
            pltpu.SMEM(positions.shape, jnp.int32),
            pltpu.VMEM(positions.shape, jnp.int32),
            pltpu.VMEM((2, rows, HD), jnp.float32),
            pltpu.VMEM((2, rows, 2 * HD), jnp.float32),
            pltpu.VMEM((2, SPAN, HD), jnp.int32),
            pltpu.VMEM((8, 128), jnp.int32),
            pltpu.SMEM((8, 128), jnp.int32),
            pltpu.SemaphoreType.DMA((4,)),
        ],
        compiler_params=pltpu.CompilerParams(vmem_limit_bytes=20 * 1024 * 1024),
        name="attend",
    )(
        *(pltpu.with_memory_space_constraint(array, pltpu.HBM) for array in (span_ids, positions)),
        queries,
        held,
    )


def combine_kernel(
    attn_ref, weight_ref, out_ref, far_out, far_in, near_out, near_in, over_out, over_in, kept,
    send_sem, recv_sem,
):
    x, zhi = lax.axis_index("tp_1"), lax.axis_index("tp_0")
    right, left, across = shifted(x=1), shifted(x=-1), shifted(z=1)
    greet([right, left, across])
    sems = (send_sem, recv_sem)
    steps = kept.shape[0]
    size = kept.shape[1]
    half = size // 2
    width = out_ref.shape[1]
    sent = []

    def share(c, dx):
        rows = attn_ref[c * size : (c + 1) * size, :]
        terms = []
        for dz in range(2):
            owner = lax.rem(zhi + dz, 2) * 4 + lax.rem(x + dx, 4)
            columns = pl.ds(pl.multiple_of(owner * width, width), width)
            terms.append(
                jnp.dot(rows, weight_ref[:, columns], preferred_element_type=jnp.float32)
            )
        return jnp.concatenate(terms, axis=1)

    def open_step(c):
        far = share(c, 2).astype(jnp.bfloat16)
        far_out[c, 0] = far[:half]
        far_out[c, 1] = far[half:]
        a = send(far_out.at[c, 0], far_in.at[c, 0], sems, c * 7, right)
        b = send(far_out.at[c, 1], far_in.at[c, 1], sems, c * 7 + 1, left)
        to_right, to_left = share(c, 1), share(c, 3)
        near_out[c, 0, 1] = to_right[half:].astype(jnp.bfloat16)
        d = send(near_out.at[c, 0, 1], near_in.at[c, 0, 1], sems, c * 7 + 2, right)
        near_out[c, 1, 0] = to_left[:half].astype(jnp.bfloat16)
        e = send(near_out.at[c, 1, 0], near_in.at[c, 1, 0], sems, c * 7 + 3, left)
        near_out[c, 0, 0] = to_right[:half].astype(jnp.bfloat16)
        near_out[c, 1, 1] = to_left[half:].astype(jnp.bfloat16)
        sent.extend((a, b, d, e))
        return a, b, d, e

    def pass_on(c, opened):
        a, b, d, e = opened
        a.wait_recv()
        near_out[c, 0, 0] = (
            near_out[c, 0, 0].astype(jnp.float32) + far_in[c, 0].astype(jnp.float32)
        ).astype(jnp.bfloat16)
        f = send(near_out.at[c, 0, 0], near_in.at[c, 0, 0], sems, c * 7 + 4, right)
        b.wait_recv()
        near_out[c, 1, 1] = (
            near_out[c, 1, 1].astype(jnp.float32) + far_in[c, 1].astype(jnp.float32)
        ).astype(jnp.bfloat16)
        g = send(near_out.at[c, 1, 1], near_in.at[c, 1, 1], sems, c * 7 + 5, left)
        sent.extend((f, g))
        return d, e, f, g

    def cross(c, passed):
        total = share(c, 0)
        for copy in passed:
            copy.wait_recv()
        for side in range(2):
            both = jnp.concatenate([near_in[c, side, 0], near_in[c, side, 1]], axis=0)
            total = total + both.astype(jnp.float32)
        over_out[c] = total[:, width:].astype(jnp.bfloat16)
        kept[c] = total[:, :width]
        copy = send(over_out.at[c], over_in.at[c], sems, c * 7 + 6, across)
        sent.append(copy)
        return copy

    def close(c, crossed):
        crossed.wait_recv()
        out_ref[c * size : (c + 1) * size, :] = (
            kept[c] + over_in[c].astype(jnp.float32)
        ).astype(jnp.bfloat16)

    opened, passed, crossed = {}, {}, {}
    for c in range(2):
        opened[c] = open_step(c)
    for c in range(steps):
        passed[c] = pass_on(c, opened[c])
        if c + 2 < steps:
            opened[c + 2] = open_step(c + 2)
        if c >= 1:
            crossed[c - 1] = cross(c - 1, passed[c - 1])
        if c >= 2:
            close(c - 2, crossed[c - 2])
    crossed[steps - 1] = cross(steps - 1, passed[steps - 1])
    close(steps - 2, crossed[steps - 2])
    close(steps - 1, crossed[steps - 1])
    for copy in sent:
        copy.wait_send()


STEPS = 4


def combine(attention, o_weight):
    vmem = pl.BlockSpec(memory_space=pltpu.VMEM)
    rows, width = attention.shape[0], o_weight.shape[1] // 8
    size = rows // STEPS
    half = (size // 2, 2 * width)
    return pl.pallas_call(
        combine_kernel,
        out_shape=jax.ShapeDtypeStruct((rows, width), jnp.bfloat16),
        in_specs=[vmem, vmem],
        out_specs=vmem,
        scratch_shapes=[
            pltpu.VMEM((STEPS, 2) + half, jnp.bfloat16),
            pltpu.VMEM((STEPS, 2) + half, jnp.bfloat16),
            pltpu.VMEM((STEPS, 2, 2) + half, jnp.bfloat16),
            pltpu.VMEM((STEPS, 2, 2) + half, jnp.bfloat16),
            pltpu.VMEM((STEPS, size, width), jnp.bfloat16),
            pltpu.VMEM((STEPS, size, width), jnp.bfloat16),
            pltpu.VMEM((STEPS, size, width), jnp.float32),
            pltpu.SemaphoreType.DMA((STEPS * 7,)),
            pltpu.SemaphoreType.DMA((STEPS * 7,)),
        ],
        compiler_params=pltpu.CompilerParams(
            collective_id=1, has_side_effects=True, vmem_limit_bytes=32 * 1024 * 1024
        ),
        name="combine",
    )(attention, o_weight)


def per_device(tokens, span_ids, positions, q_weight, k_weight, v_weight, o_weight):
    lines = positions.reshape(CHUNKS, ROWS)
    queries, held = project(span_ids, lines, tokens, q_weight, k_weight, v_weight)
    attention = attend(span_ids, lines, queries, held.reshape(-1, BLOCK, HD))
    return combine(attention, o_weight)


def solution(mesh):
    split = Mesh(mesh.devices.reshape(4, 4, 2, 2, 4), ("cp_0", "cp_1", "cp_2", "tp_0", "tp_1"))
    placed = (P(CP, TP), P(CP, None), P(CP), P(None, TP), P(None, TP), P(None, TP), P(TP, None))
    return jax.shard_map(
        per_device, mesh=split, in_specs=placed, out_specs=P(CP, TP), check_vma=False
    )
```

```python
import jax
import jax.numpy as jnp
from jax import lax
from jax.experimental import pallas as pl
from jax.experimental.pallas import tpu as pltpu
from jax.sharding import Mesh
from jax.sharding import PartitionSpec as P

HD = 128
SPAN = 256
LOG2E = 1.4426950408889634
TP = ("tp_0", "tp_1")
CP = ("cp_0", "cp_1", "cp_2")


theta_base = 500000.0
floor_score = -1e30


MESH = pl.DeviceIdType.MESH
CHUNKS = 4
ROWS = 128
TAG = 2 * ROWS
BLOCK = TAG + 16


def shifted(x=0, y=0, z=0, row=0, other_core=False):
    place = {}
    if x:
        place["tp_1"] = lax.rem(lax.axis_index("tp_1") + x + 4, 4)
    if y:
        place["cp_1"] = lax.rem(lax.axis_index("cp_1") + y + 4, 4)
    if z:
        place["tp_0"] = 1 - lax.axis_index("tp_0")
    if row:
        place["cp_0"] = lax.rem(lax.axis_index("cp_0") + row + 4, 4)
    if other_core:
        place["cp_2"] = 1 - lax.axis_index("cp_2")
    return place


def greet(peers):
    barrier = pltpu.get_barrier_semaphore()
    for peer in peers:
        pl.semaphore_signal(barrier, inc=1, device_id=peer, device_id_type=MESH)
    pl.semaphore_wait(barrier, len(peers))


def sending(source, target, sems, index, peer, arrival=None):
    return pltpu.make_async_remote_copy(
        src_ref=source,
        dst_ref=target,
        send_sem=sems[0].at[index],
        recv_sem=sems[1].at[index if arrival is None else arrival],
        device_id=peer,
        device_id_type=MESH,
    )


def send(source, target, sems, index, peer):
    copy = sending(source, target, sems, index, peer)
    copy.start()
    return copy


def columns_of(line):
    return jnp.broadcast_to(line, (128, 128)).T


def turn_table(line):
    lane = lax.rem(lax.broadcasted_iota(jnp.int32, (8, 128), 1), HD // 2)
    frequency = jnp.zeros((8, 128), jnp.float32)
    for j in range(HD // 2):
        frequency = jnp.where(lane == j, theta_base ** (-2.0 * j / HD), frequency)
    angle = columns_of(line.astype(jnp.float32)) * frequency[:1]
    turns = jnp.floor(angle * 0.6366197723675814 + 0.5)
    rest = ((angle - turns * 1.5703125) - turns * 4.837512969970703e-4) - turns * 7.549789954891882e-8
    square = rest * rest
    cosine = (2.443315711809948e-5 * square - 1.388731625493765e-3) * square + 4.166664568298827e-2
    cosine = cosine * square * square - 0.5 * square + 1.0
    sine = (-1.9515295891e-4 * square + 8.3321608736e-3) * square - 1.6666654611e-1
    sine = sine * square * rest + rest
    quarter = turns - 4.0 * jnp.floor(turns * 0.25)
    odd = (quarter == 1.0) | (quarter == 3.0)
    cos_all = jnp.where(odd, sine, cosine)
    sin_all = jnp.where(odd, cosine, sine)
    cos_all = jnp.where((quarter == 1.0) | (quarter == 2.0), -cos_all, cos_all)
    sin_all = jnp.where(quarter >= 2.0, -sin_all, sin_all)
    side = lax.broadcasted_iota(jnp.int32, (128, 128), 1)
    return cos_all, jnp.where(side < HD // 2, -sin_all, sin_all)


ORDER = (
    "n0", "a0", "n1", "f0", "a1", "d0", "x0", "n2", "f1", "n3",
    "a2", "d1", "x1", "s0", "f2", "a3", "d2", "x2", "s1", "w0",
    "f3", "d3", "l0", "x3", "s2", "w1", "s3", "w2", "l1", "w3",
    "l2", "l3",
)
TOKEN_SEMS = 9
KEY_SEMS = 20


def project_kernel(
    ids_hbm,
    positions_hbm,
    tokens_hbm,
    wq_hbm,
    wk_hbm,
    wv_hbm,
    q_ref,
    kv_ref,
    ids_ref,
    positions_ref,
    tokens_ref,
    wq_ref,
    wk_ref,
    wv_ref,
    held,
    load_sem,
    token_send,
    token_recv,
    key_send,
    key_recv,
):
    x, zhi = lax.axis_index("tp_1"), lax.axis_index("tp_0")
    row, y, core = lax.axis_index("cp_0"), lax.axis_index("cp_1"), lax.axis_index("cp_2")
    loads = [
        pltpu.make_async_copy(a, b, load_sem.at[i])
        for i, (a, b) in enumerate(
            (
                (tokens_hbm, tokens_ref),
                (ids_hbm, ids_ref),
                (positions_hbm, positions_ref),
                (wk_hbm, wk_ref),
                (wv_hbm, wv_ref),
                (wq_hbm, wq_ref),
            )
        )
    ]
    for load in loads:
        load.start()
    right, left, across = shifted(x=1), shifted(x=-1), shifted(z=1)
    up, down, mate = shifted(y=1), shifted(y=-1), shifted(other_core=True)
    rows_of = [shifted(row=d) for d in (1, 2, 3)]
    greet([right, left, across, up, down, mate] + rows_of)
    tok, key = (token_send, token_recv), (key_send, key_recv)
    sent = []
    half = ROWS // 2
    inner = (row == 1) | (row == 2)
    loads[0].wait()

    def token_rows(c, part=None):
        if part is None:
            return pl.ds(c * ROWS, ROWS)
        return pl.ds(c * ROWS + part * half, half)

    def across_send(c):
        rows = token_rows(c)
        copy = send(
            tokens_ref.at[rows], held.at[1, 0, rows], tok, c * TOKEN_SEMS + 8, across
        )
        sent.append(copy)
        return copy

    def side_sends(c, dz):
        rows = token_rows(c)
        source = held.at[1, 0, rows] if dz else tokens_ref.at[rows]
        a = send(source, held.at[dz, 3, rows], tok, c * TOKEN_SEMS + dz * 4, right)
        b = send(source, held.at[dz, 1, rows], tok, c * TOKEN_SEMS + dz * 4 + 1, left)
        sent.extend((a, b))
        return a, b

    def side_forwards(c, dz):
        at = c * TOKEN_SEMS + dz * 4
        rows = token_rows(c, 0)
        a = send(held.at[dz, 3, rows], held.at[dz, 2, rows], tok, at + 2, right)
        rows = token_rows(c, 1)
        b = send(held.at[dz, 1, rows], held.at[dz, 2, rows], tok, at + 3, left)
        sent.extend((a, b))
        return a, b

    def product(c, dz, dx):
        owner = lax.rem(zhi + dz, 2) * 4 + lax.rem(x + dx, 4)
        rows = pl.ds(pl.multiple_of(owner * 512, 512), 512)
        weights = jnp.concatenate([wk_ref[rows, :], wv_ref[rows, :], wq_ref[rows, :]], axis=1)
        if dz == 0 and dx == 0:
            features = tokens_ref[token_rows(c), :]
        else:
            features = held[dz, dx, token_rows(c), :]
        return jnp.dot(features, weights, preferred_element_type=jnp.float32)

    def key_rows(c):
        at = c * KEY_SEMS
        block = kv_ref.at[c, core, y, row]
        out = []
        for d, skip in ((1, row == 3), (2, None), (3, row == 0)):
            copy = sending(block, block, key, at + d - 1, rows_of[d - 1])
            if skip is None:
                copy.start()
            else:
                pl.when(jnp.logical_not(skip))(copy.start)
            out.append(copy)
        return out, [key_side(c, 0)]

    def key_side(c, d):
        block = kv_ref.at[c, core, y, lax.rem(row + 4 - d, 4)]
        a = send(block, block, key, c * KEY_SEMS + 4 + d, up)
        b = send(block, block, key, c * KEY_SEMS + 8 + d, down)
        sent.extend((a, b))
        return a, b

    def key_relay(c):
        at = c * KEY_SEMS
        block = kv_ref.at[c, core, y, lax.rem(row + 2, 4)]
        end = {"cp_0": jnp.where(row == 2, 3, 0)}
        arrival = at + jnp.where(row == 2, 2, 0)
        return sending(block, block, key, at + 3, end, arrival)

    def key_sides(c, started):
        out, sides = started
        relay = key_relay(c)
        out[1].wait_recv()
        pl.when(inner)(relay.start)
        sides.append(key_side(c, 2))
        out[0].wait_recv()
        sides.append(key_side(c, 1))
        out[2].wait_recv()
        sides.append(key_side(c, 3))
        mine = kv_ref.at[c, core, y]
        m = send(mine, mine, key, c * KEY_SEMS + 16, mate)
        sent.append(m)
        return sides, m, relay

    def key_forwards(c, state):
        sides, m, relay = state
        at = c * KEY_SEMS
        behind, ahead = lax.rem(y + 3, 4), lax.rem(y + 1, 4)
        forwards = []
        for place, d in enumerate((0, 2, 1, 3)):
            a, b = sides[place]
            block_at = lax.rem(row + 4 - d, 4)
            a.wait_recv()
            b.wait_recv()
            if d in (0, 1):
                block = kv_ref.at[c, core, behind, block_at]
                f = send(block, block, key, at + 12 + d, up)
            else:
                block = kv_ref.at[c, core, ahead, block_at]
                f = send(block, block, key, at + 12 + d, down)
            forwards.append(f)
        mates = [m]
        for i, at_y in enumerate((behind, ahead)):
            got = kv_ref.at[c, core, at_y]
            mates.append(send(got, got, key, at + 17 + i, mate))
        sent.extend(forwards + mates[1:])
        return forwards, mates

    def key_last(c, moved):
        forwards, mates = moved
        for f in forwards:
            f.wait_recv()
        got = kv_ref.at[c, core, lax.rem(y + 2, 4)]
        mc = send(got, got, key, c * KEY_SEMS + 19, mate)
        sent.append(mc)
        return mates + [mc]

    across_of, own_of, far_of, near_on, far_on = {}, {}, {}, {}, {}
    rows_at, sides_at, moved_at, totals, mates = {}, {}, {}, {}, []

    def near_step(c):
        for copy in own_of[c]:
            copy.wait_recv()
        near_on[c] = side_forwards(c, 0)

    def across_step(c):
        if c < CHUNKS:
            across_of[c].wait_recv()
            far_of[c] = side_sends(c, 1)

    def far_step(c):
        if c < CHUNKS:
            for copy in far_of[c]:
                copy.wait_recv()
            far_on[c] = side_forwards(c, 1)

    def multiply(c):
        total = product(c, 0, 0)
        for dz, dx in ((0, 3), (0, 1), (1, 0), (1, 3), (1, 1)):
            total = total + product(c, dz, dx)
        totals[c] = total

    def finish(c):
        total = totals[c]
        cosine, sine = turn_table(positions_ref[c : c + 1, :])
        for copy in near_on[c]:
            copy.wait_recv()
        total = total + product(c, 0, 2)
        for copy in far_on[c]:
            copy.wait_recv()
        total = total + product(c, 1, 2)

        def turned(vectors):
            return (vectors * cosine + pltpu.roll(vectors, HD // 2, 1) * sine).astype(jnp.bfloat16)

        kv_ref[c, core, y, row, :ROWS, :] = turned(total[:, :HD])
        kv_ref[c, core, y, row, ROWS:TAG, :] = total[:, HD : 2 * HD].astype(jnp.bfloat16)
        tag = ids_ref[0, c // 2].astype(jnp.float32)
        kv_ref[c, core, y, row, TAG:, :] = jnp.full((16, HD), tag, jnp.float32).astype(jnp.bfloat16)
        rows_at[c] = key_rows(c)
        for head in range(4):
            at = head * SPAN + (c % 2) * ROWS
            q_ref[c // 2, at : at + ROWS, :] = turned(total[:, (2 + head) * HD : (3 + head) * HD])

    def side_step(c):
        sides_at[c] = key_sides(c, rows_at[c])

    def forward_step(c):
        moved_at[c] = key_forwards(c, sides_at[c])

    def last_step(c):
        mates.extend(key_last(c, moved_at[c]))

    for c in range(CHUNKS):
        own_of[c] = side_sends(c, 0)
        across_of[c] = across_send(c)
    actions = {
        "n": near_step,
        "a": across_step,
        "f": far_step,
        "d": multiply,
        "x": finish,
        "s": side_step,
        "w": forward_step,
        "l": last_step,
    }
    for action in ORDER:
        if action == "d0":
            for load in loads[1:]:
                load.wait()
        actions[action[0]](int(action[1:]))
    for copy in mates:
        copy.wait_recv()
    for copy in sent:
        copy.wait_send()
    for c in range(CHUNKS):
        out = rows_at[c][0]
        out[1].wait_send()
        pl.when(row != 3)(out[0].wait_send)
        pl.when(row != 0)(out[2].wait_send)
        pl.when(inner)(sides_at[c][2].wait_send)


def project(span_ids, positions, tokens, q_weight, k_weight, v_weight):
    vmem = pl.BlockSpec(memory_space=pltpu.VMEM)
    hbm = pl.BlockSpec(memory_space=pltpu.HBM)
    return pl.pallas_call(
        project_kernel,
        out_shape=(
            jax.ShapeDtypeStruct((2, 4 * SPAN, HD), jnp.bfloat16),
            jax.ShapeDtypeStruct((CHUNKS, 2, 4, 4, BLOCK, HD), jnp.bfloat16),
        ),
        in_specs=[hbm] * 6,
        out_specs=(vmem, vmem),
        scratch_shapes=[
            pltpu.SMEM(span_ids.shape, jnp.int32),
            pltpu.VMEM(positions.shape, jnp.int32),
            pltpu.VMEM(tokens.shape, jnp.bfloat16),
            pltpu.VMEM(q_weight.shape, jnp.bfloat16),
            pltpu.VMEM(k_weight.shape, jnp.bfloat16),
            pltpu.VMEM(v_weight.shape, jnp.bfloat16),
            pltpu.VMEM((2, 4) + tokens.shape, jnp.bfloat16),
            pltpu.SemaphoreType.DMA((6,)),
            pltpu.SemaphoreType.DMA((CHUNKS * TOKEN_SEMS,)),
            pltpu.SemaphoreType.DMA((CHUNKS * TOKEN_SEMS,)),
            pltpu.SemaphoreType.DMA((CHUNKS * KEY_SEMS,)),
            pltpu.SemaphoreType.DMA((CHUNKS * KEY_SEMS,)),
        ],
        compiler_params=pltpu.CompilerParams(
            collective_id=0, has_side_effects=True, vmem_limit_bytes=26 * 1024 * 1024
        ),
        name="project",
    )(
        *(
            pltpu.with_memory_space_constraint(array, pltpu.HBM)
            for array in (span_ids, positions, tokens, q_weight, k_weight, v_weight)
        )
    )


def attend_kernel(
    ids_hbm, positions_hbm, q_ref, kv_ref, out_ref, ids, places_of, positions_ref, top_ref, acc_ref,
    start_ref, table_ref, where, sems,
):
    loads = [
        pltpu.make_async_copy(a, b, sems.at[i + 1])
        for i, (a, b) in enumerate(
            ((ids_hbm, ids), (positions_hbm, positions_ref), (positions_hbm, places_of))
        )
    ]
    for load in loads:
        load.start()
    heads = q_ref.shape[1] // SPAN
    scale = LOG2E * HD**-0.5
    ones = jnp.ones((SPAN, HD), jnp.bfloat16)
    lane = lax.broadcasted_iota(jnp.int32, (8, 128), 1).astype(jnp.float32)
    table = jnp.zeros((8, 128), jnp.int32)
    for block in range(64):
        at = (block // 32) * 64 + block % 32
        tag = kv_ref[at, TAG:, :].astype(jnp.float32)[:8]
        table = table + jnp.where(tag == lane, block, 0)
    table_ref[...] = table
    fetch = pltpu.make_async_copy(table_ref, where, sems.at[0])
    fetch.start()
    row, y, core = lax.axis_index("cp_0"), lax.axis_index("cp_1"), lax.axis_index("cp_2")
    home = core * 16 + y * 4 + row
    for load in loads:
        load.wait()
    for half in range(2):
        own = ids[0, half]
        for part in range(2):
            line = 2 * half + part
            column = columns_of(positions_ref[line : line + 1, :].astype(jnp.float32))
            place = own * SPAN + part * 128
            place = place + lax.broadcasted_iota(jnp.int32, (128, 128), 0)
            start_ref[half, part * 128 : (part + 1) * 128, :] = place - column.astype(jnp.int32)

    def block(half, span, place, masked, first):
        first_place = (place // 32) * 64 + lax.rem(place, 32)
        places = (first_place, first_place + 32)
        keys = jnp.concatenate([kv_ref[at, :ROWS, :] for at in places], axis=0)
        values = jnp.concatenate([kv_ref[at, ROWS:TAG, :] for at in places], axis=0)
        values = jnp.concatenate([values, ones], axis=1)
        if masked:
            key = span * SPAN + lax.broadcasted_iota(jnp.int32, (SPAN, SPAN), 1)
            start = start_ref[half]
            seen = key >= jnp.concatenate([start, start], axis=1)
            if first:
                query = span * SPAN + lax.broadcasted_iota(jnp.int32, (SPAN, SPAN), 0)
                seen = seen & (key <= query)
        for head in range(heads):
            rows = slice(head * SPAN, (head + 1) * SPAN)
            score = lax.dot_general(
                q_ref[half, rows, :],
                keys,
                (((1,), (1,)), ((), ())),
                preferred_element_type=jnp.float32,
            )
            score = score * scale
            if masked:
                score = jnp.where(seen, score, floor_score)
            top = jnp.max(score, axis=1, keepdims=True)
            if first:
                weight = jnp.exp2(score - top)
                top_ref[half, rows, :] = jnp.broadcast_to(top, (SPAN, HD))
            else:
                before = top_ref[half, rows, :]
                now = jnp.maximum(before, top)
                weight = jnp.exp2(score - jnp.concatenate([now, now], axis=1))
                fade = jnp.exp2(before - now)
                top_ref[half, rows, :] = now
            mixed = jnp.dot(
                weight.astype(jnp.bfloat16), values, preferred_element_type=jnp.float32
            )
            if not first:
                mixed = mixed + acc_ref[half, rows, :] * jnp.concatenate([fade, fade], axis=1)
            acc_ref[half, rows, :] = mixed

    for half in range(2):
        block(half, ids[0, half], home + 32 * half, True, True)
    fetch.wait()
    for half in range(2):
        own = ids[0, half]
        low = (own * SPAN - places_of[2 * half, 0]) // SPAN
        clear = (own * SPAN + 2 * SPAN - 2 - places_of[2 * half + 1, 127]) // SPAN
        clear = jnp.minimum(clear, own)

        def masked_step(span, carry):
            block(half, span, where[0, span], True, False)
            return carry

        def clear_step(span, carry):
            block(half, span, where[0, span], False, False)
            return carry

        lax.fori_loop(low, clear, masked_step, 0)
        lax.fori_loop(clear, own, clear_step, 0)
        for head in range(heads):
            rows = slice(head * SPAN, (head + 1) * SPAN)
            mixed = acc_ref[half, rows, :HD] / acc_ref[half, rows, HD:]
            out_ref[half * SPAN : (half + 1) * SPAN, head * HD : (head + 1) * HD] = mixed.astype(
                jnp.bfloat16
            )


def attend(span_ids, positions, queries, held):
    vmem = pl.BlockSpec(memory_space=pltpu.VMEM)
    hbm = pl.BlockSpec(memory_space=pltpu.HBM)
    rows = queries.shape[1]
    heads = rows // SPAN
    return pl.pallas_call(
        attend_kernel,
        out_shape=jax.ShapeDtypeStruct((2 * SPAN, heads * HD), jnp.bfloat16),
        in_specs=[hbm, hbm, vmem, vmem],
        out_specs=vmem,
        scratch_shapes=[
            pltpu.SMEM(span_ids.shape, jnp.int32),
            pltpu.SMEM(positions.shape, jnp.int32),
            pltpu.VMEM(positions.shape, jnp.int32),
            pltpu.VMEM((2, rows, HD), jnp.float32),
            pltpu.VMEM((2, rows, 2 * HD), jnp.float32),
            pltpu.VMEM((2, SPAN, HD), jnp.int32),
            pltpu.VMEM((8, 128), jnp.int32),
            pltpu.SMEM((8, 128), jnp.int32),
            pltpu.SemaphoreType.DMA((4,)),
        ],
        compiler_params=pltpu.CompilerParams(vmem_limit_bytes=20 * 1024 * 1024),
        name="attend",
    )(
        *(pltpu.with_memory_space_constraint(array, pltpu.HBM) for array in (span_ids, positions)),
        queries,
        held,
    )


STEPS = 4
COMBINE_ORDER = (
    "o0", "o1", "p0", "o2", "o3", "p1", "p2", "p3", "c0", "c1",
    "c2", "c3", "e0", "e1", "e2", "e3",
)


def combine_kernel(
    attn_ref, weight_ref, out_ref, far_out, far_in, near_out, near_in, over_out, over_in, kept,
    send_sem, recv_sem,
):
    x, zhi = lax.axis_index("tp_1"), lax.axis_index("tp_0")
    right, left, across = shifted(x=1), shifted(x=-1), shifted(z=1)
    greet([right, left, across])
    sems = (send_sem, recv_sem)
    steps = kept.shape[0]
    size = kept.shape[1]
    half = size // 2
    width = out_ref.shape[1]
    sent = []

    def share(c, dx):
        rows = attn_ref[c * size : (c + 1) * size, :]
        terms = []
        for dz in range(2):
            owner = lax.rem(zhi + dz, 2) * 4 + lax.rem(x + dx, 4)
            columns = pl.ds(pl.multiple_of(owner * width, width), width)
            terms.append(
                jnp.dot(rows, weight_ref[:, columns], preferred_element_type=jnp.float32)
            )
        return jnp.concatenate(terms, axis=1)

    def open_step(c):
        far = share(c, 2).astype(jnp.bfloat16)
        far_out[c, 0] = far[:half]
        far_out[c, 1] = far[half:]
        a = send(far_out.at[c, 0], far_in.at[c, 0], sems, c * 7, right)
        b = send(far_out.at[c, 1], far_in.at[c, 1], sems, c * 7 + 1, left)
        to_right, to_left = share(c, 1), share(c, 3)
        near_out[c, 0, 1] = to_right[half:].astype(jnp.bfloat16)
        d = send(near_out.at[c, 0, 1], near_in.at[c, 0, 1], sems, c * 7 + 2, right)
        near_out[c, 1, 0] = to_left[:half].astype(jnp.bfloat16)
        e = send(near_out.at[c, 1, 0], near_in.at[c, 1, 0], sems, c * 7 + 3, left)
        near_out[c, 0, 0] = to_right[:half].astype(jnp.bfloat16)
        near_out[c, 1, 1] = to_left[half:].astype(jnp.bfloat16)
        sent.extend((a, b, d, e))
        return a, b, d, e

    def pass_on(c, opened):
        a, b, d, e = opened
        a.wait_recv()
        near_out[c, 0, 0] = (
            near_out[c, 0, 0].astype(jnp.float32) + far_in[c, 0].astype(jnp.float32)
        ).astype(jnp.bfloat16)
        f = send(near_out.at[c, 0, 0], near_in.at[c, 0, 0], sems, c * 7 + 4, right)
        b.wait_recv()
        near_out[c, 1, 1] = (
            near_out[c, 1, 1].astype(jnp.float32) + far_in[c, 1].astype(jnp.float32)
        ).astype(jnp.bfloat16)
        g = send(near_out.at[c, 1, 1], near_in.at[c, 1, 1], sems, c * 7 + 5, left)
        sent.extend((f, g))
        return d, e, f, g

    def cross(c, passed):
        total = share(c, 0)
        for copy in passed:
            copy.wait_recv()
        for side in range(2):
            both = jnp.concatenate([near_in[c, side, 0], near_in[c, side, 1]], axis=0)
            total = total + both.astype(jnp.float32)
        over_out[c] = total[:, width:].astype(jnp.bfloat16)
        kept[c] = total[:, :width]
        copy = send(over_out.at[c], over_in.at[c], sems, c * 7 + 6, across)
        sent.append(copy)
        return copy

    def close(c, crossed):
        crossed.wait_recv()
        out_ref[c * size : (c + 1) * size, :] = (
            kept[c] + over_in[c].astype(jnp.float32)
        ).astype(jnp.bfloat16)

    opened, passed, crossed = {}, {}, {}
    for action in COMBINE_ORDER:
        c = int(action[1])
        if action[0] == "o":
            opened[c] = open_step(c)
        elif action[0] == "p":
            passed[c] = pass_on(c, opened[c])
        elif action[0] == "c":
            crossed[c] = cross(c, passed[c])
        else:
            close(c, crossed[c])
    for copy in sent:
        copy.wait_send()


def combine(attention, o_weight):
    vmem = pl.BlockSpec(memory_space=pltpu.VMEM)
    rows, width = attention.shape[0], o_weight.shape[1] // 8
    size = rows // STEPS
    half = (size // 2, 2 * width)
    return pl.pallas_call(
        combine_kernel,
        out_shape=jax.ShapeDtypeStruct((rows, width), jnp.bfloat16),
        in_specs=[vmem, vmem],
        out_specs=vmem,
        scratch_shapes=[
            pltpu.VMEM((STEPS, 2) + half, jnp.bfloat16),
            pltpu.VMEM((STEPS, 2) + half, jnp.bfloat16),
            pltpu.VMEM((STEPS, 2, 2) + half, jnp.bfloat16),
            pltpu.VMEM((STEPS, 2, 2) + half, jnp.bfloat16),
            pltpu.VMEM((STEPS, size, width), jnp.bfloat16),
            pltpu.VMEM((STEPS, size, width), jnp.bfloat16),
            pltpu.VMEM((STEPS, size, width), jnp.float32),
            pltpu.SemaphoreType.DMA((STEPS * 7,)),
            pltpu.SemaphoreType.DMA((STEPS * 7,)),
        ],
        compiler_params=pltpu.CompilerParams(
            collective_id=1, has_side_effects=True, vmem_limit_bytes=32 * 1024 * 1024
        ),
        name="combine",
    )(attention, o_weight)


def per_device(tokens, span_ids, positions, q_weight, k_weight, v_weight, o_weight):
    lines = positions.reshape(CHUNKS, ROWS)
    queries, held = project(span_ids, lines, tokens, q_weight, k_weight, v_weight)
    attention = attend(span_ids, lines, queries, held.reshape(-1, BLOCK, HD))
    return combine(attention, o_weight)


def solution(mesh):
    split = Mesh(mesh.devices.reshape(4, 4, 2, 2, 4), ("cp_0", "cp_1", "cp_2", "tp_0", "tp_1"))
    placed = (P(CP, TP), P(CP, None), P(CP), P(None, TP), P(None, TP), P(None, TP), P(TP, None))
    return jax.shard_map(
        per_device, mesh=split, in_specs=placed, out_specs=P(CP, TP), check_vma=False
    )
```

```python
import jax
import jax.numpy as jnp
from jax import lax
from jax.experimental import pallas as pl
from jax.experimental.pallas import tpu as pltpu
from jax.sharding import Mesh
from jax.sharding import PartitionSpec as P

HD = 128
SPAN = 256
LOG2E = 1.4426950408889634
TP = ("tp_0", "tp_1")
CP = ("cp_0", "cp_1", "cp_2")


theta_base = 500000.0
floor_score = -1e30


MESH = pl.DeviceIdType.MESH
CHUNKS = 4
ROWS = 128
TAG = 2 * ROWS
BLOCK = TAG + 16


def shifted(x=0, y=0, z=0, row=0, other_core=False):
    place = {}
    if x:
        place["tp_1"] = lax.rem(lax.axis_index("tp_1") + x + 4, 4)
    if y:
        place["cp_1"] = lax.rem(lax.axis_index("cp_1") + y + 4, 4)
    if z:
        place["tp_0"] = 1 - lax.axis_index("tp_0")
    if row:
        place["cp_0"] = lax.rem(lax.axis_index("cp_0") + row + 4, 4)
    if other_core:
        place["cp_2"] = 1 - lax.axis_index("cp_2")
    return place


def greet(peers):
    barrier = pltpu.get_barrier_semaphore()
    for peer in peers:
        pl.semaphore_signal(barrier, inc=1, device_id=peer, device_id_type=MESH)
    pl.semaphore_wait(barrier, len(peers))


def sending(source, target, sems, index, peer, arrival=None):
    return pltpu.make_async_remote_copy(
        src_ref=source,
        dst_ref=target,
        send_sem=sems[0].at[index],
        recv_sem=sems[1].at[index if arrival is None else arrival],
        device_id=peer,
        device_id_type=MESH,
    )


def send(source, target, sems, index, peer):
    copy = sending(source, target, sems, index, peer)
    copy.start()
    return copy


def columns_of(line):
    return jnp.broadcast_to(line, (128, 128)).T


def turn_table(line):
    lane = lax.rem(lax.broadcasted_iota(jnp.int32, (8, 128), 1), HD // 2)
    frequency = jnp.zeros((8, 128), jnp.float32)
    for j in range(HD // 2):
        frequency = jnp.where(lane == j, theta_base ** (-2.0 * j / HD), frequency)
    angle = columns_of(line.astype(jnp.float32)) * frequency[:1]
    turns = jnp.floor(angle * 0.6366197723675814 + 0.5)
    rest = ((angle - turns * 1.5703125) - turns * 4.837512969970703e-4) - turns * 7.549789954891882e-8
    square = rest * rest
    cosine = (2.443315711809948e-5 * square - 1.388731625493765e-3) * square + 4.166664568298827e-2
    cosine = cosine * square * square - 0.5 * square + 1.0
    sine = (-1.9515295891e-4 * square + 8.3321608736e-3) * square - 1.6666654611e-1
    sine = sine * square * rest + rest
    quarter = turns - 4.0 * jnp.floor(turns * 0.25)
    odd = (quarter == 1.0) | (quarter == 3.0)
    cos_all = jnp.where(odd, sine, cosine)
    sin_all = jnp.where(odd, cosine, sine)
    cos_all = jnp.where((quarter == 1.0) | (quarter == 2.0), -cos_all, cos_all)
    sin_all = jnp.where(quarter >= 2.0, -sin_all, sin_all)
    side = lax.broadcasted_iota(jnp.int32, (128, 128), 1)
    return cos_all, jnp.where(side < HD // 2, -sin_all, sin_all)


ORDER = (
    "n0", "a0", "n1", "f0", "a1", "d0", "x0", "n2", "f1", "n3",
    "a2", "d1", "x1", "s0", "f2", "a3", "d2", "x2", "s1", "w0",
    "f3", "d3", "l0", "x3", "s2", "w1", "s3", "w2", "l1", "w3",
    "l2", "l3",
)
TOKEN_SEMS = 9
KEY_SEMS = 20


def project_kernel(
    ids_hbm,
    positions_hbm,
    tokens_hbm,
    wq_hbm,
    wk_hbm,
    wv_hbm,
    q_ref,
    kv_ref,
    ids_ref,
    positions_ref,
    tokens_ref,
    wq_ref,
    wk_ref,
    wv_ref,
    held,
    load_sem,
    token_send,
    token_recv,
    key_send,
    key_recv,
):
    x, zhi = lax.axis_index("tp_1"), lax.axis_index("tp_0")
    row, y, core = lax.axis_index("cp_0"), lax.axis_index("cp_1"), lax.axis_index("cp_2")
    loads = [
        pltpu.make_async_copy(a, b, load_sem.at[i])
        for i, (a, b) in enumerate(
            (
                (tokens_hbm, tokens_ref),
                (ids_hbm, ids_ref),
                (positions_hbm, positions_ref),
                (wk_hbm, wk_ref),
                (wv_hbm, wv_ref),
                (wq_hbm, wq_ref),
            )
        )
    ]
    for load in loads:
        load.start()
    right, left, across = shifted(x=1), shifted(x=-1), shifted(z=1)
    up, down, mate = shifted(y=1), shifted(y=-1), shifted(other_core=True)
    rows_of = [shifted(row=d) for d in (1, 2, 3)]
    greet([right, left, across, up, down, mate] + rows_of)
    tok, key = (token_send, token_recv), (key_send, key_recv)
    sent = []
    half = ROWS // 2
    inner = (row == 1) | (row == 2)
    loads[0].wait()

    def token_rows(c, part=None):
        if part is None:
            return pl.ds(c * ROWS, ROWS)
        return pl.ds(c * ROWS + part * half, half)

    def across_send(c):
        rows = token_rows(c)
        copy = send(
            tokens_ref.at[rows], held.at[1, 0, rows], tok, c * TOKEN_SEMS + 8, across
        )
        sent.append(copy)
        return copy

    def side_sends(c, dz):
        rows = token_rows(c)
        source = held.at[1, 0, rows] if dz else tokens_ref.at[rows]
        a = send(source, held.at[dz, 3, rows], tok, c * TOKEN_SEMS + dz * 4, right)
        b = send(source, held.at[dz, 1, rows], tok, c * TOKEN_SEMS + dz * 4 + 1, left)
        sent.extend((a, b))
        return a, b

    def side_forwards(c, dz):
        at = c * TOKEN_SEMS + dz * 4
        rows = token_rows(c, 0)
        a = send(held.at[dz, 3, rows], held.at[dz, 2, rows], tok, at + 2, right)
        rows = token_rows(c, 1)
        b = send(held.at[dz, 1, rows], held.at[dz, 2, rows], tok, at + 3, left)
        sent.extend((a, b))
        return a, b

    def product(c, dz, dx):
        owner = lax.rem(zhi + dz, 2) * 4 + lax.rem(x + dx, 4)
        rows = pl.ds(pl.multiple_of(owner * 512, 512), 512)
        weights = jnp.concatenate([wk_ref[rows, :], wv_ref[rows, :], wq_ref[rows, :]], axis=1)
        if dz == 0 and dx == 0:
            features = tokens_ref[token_rows(c), :]
        else:
            features = held[dz, dx, token_rows(c), :]
        return jnp.dot(features, weights, preferred_element_type=jnp.float32)

    def key_rows(c):
        at = c * KEY_SEMS
        block = kv_ref.at[c, core, y, row]
        out = []
        for d, skip in ((1, row == 3), (2, None), (3, row == 0)):
            copy = sending(block, block, key, at + d - 1, rows_of[d - 1])
            if skip is None:
                copy.start()
            else:
                pl.when(jnp.logical_not(skip))(copy.start)
            out.append(copy)
        return out, [key_side(c, 0)]

    def key_side(c, d):
        block = kv_ref.at[c, core, y, lax.rem(row + 4 - d, 4)]
        a = send(block, block, key, c * KEY_SEMS + 4 + d, up)
        b = send(block, block, key, c * KEY_SEMS + 8 + d, down)
        sent.extend((a, b))
        return a, b

    def key_relay(c):
        at = c * KEY_SEMS
        block = kv_ref.at[c, core, y, lax.rem(row + 2, 4)]
        end = {"cp_0": jnp.where(row == 2, 3, 0)}
        arrival = at + jnp.where(row == 2, 2, 0)
        return sending(block, block, key, at + 3, end, arrival)

    def key_sides(c, started):
        out, sides = started
        relay = key_relay(c)
        out[1].wait_recv()
        pl.when(inner)(relay.start)
        sides.append(key_side(c, 2))
        out[0].wait_recv()
        sides.append(key_side(c, 1))
        out[2].wait_recv()
        sides.append(key_side(c, 3))
        mine = kv_ref.at[c, core, y]
        m = send(mine, mine, key, c * KEY_SEMS + 16, mate)
        sent.append(m)
        return sides, m, relay

    def key_forwards(c, state):
        sides, m, relay = state
        at = c * KEY_SEMS
        behind, ahead = lax.rem(y + 3, 4), lax.rem(y + 1, 4)
        forwards = []
        for place, d in enumerate((0, 2, 1, 3)):
            a, b = sides[place]
            block_at = lax.rem(row + 4 - d, 4)
            a.wait_recv()
            b.wait_recv()
            if d in (0, 1):
                block = kv_ref.at[c, core, behind, block_at]
                f = send(block, block, key, at + 12 + d, up)
            else:
                block = kv_ref.at[c, core, ahead, block_at]
                f = send(block, block, key, at + 12 + d, down)
            forwards.append(f)
        mates = [m]
        for i, at_y in enumerate((behind, ahead)):
            got = kv_ref.at[c, core, at_y]
            mates.append(send(got, got, key, at + 17 + i, mate))
        sent.extend(forwards + mates[1:])
        return forwards, mates

    def key_last(c, moved):
        forwards, mates = moved
        for f in forwards:
            f.wait_recv()
        got = kv_ref.at[c, core, lax.rem(y + 2, 4)]
        mc = send(got, got, key, c * KEY_SEMS + 19, mate)
        sent.append(mc)
        return mates + [mc]

    across_of, own_of, far_of, near_on, far_on = {}, {}, {}, {}, {}
    rows_at, sides_at, moved_at, totals, mates = {}, {}, {}, {}, []

    def near_step(c):
        for copy in own_of[c]:
            copy.wait_recv()
        near_on[c] = side_forwards(c, 0)

    def across_step(c):
        if c < CHUNKS:
            across_of[c].wait_recv()
            far_of[c] = side_sends(c, 1)

    def far_step(c):
        if c < CHUNKS:
            for copy in far_of[c]:
                copy.wait_recv()
            far_on[c] = side_forwards(c, 1)

    def multiply(c):
        total = product(c, 0, 0)
        for dz, dx in ((0, 3), (0, 1), (1, 0), (1, 3), (1, 1)):
            total = total + product(c, dz, dx)
        totals[c] = total

    def finish(c):
        total = totals[c]
        cosine, sine = turn_table(positions_ref[c : c + 1, :])
        for copy in near_on[c]:
            copy.wait_recv()
        total = total + product(c, 0, 2)
        for copy in far_on[c]:
            copy.wait_recv()
        total = total + product(c, 1, 2)

        def turned(vectors):
            return (vectors * cosine + pltpu.roll(vectors, HD // 2, 1) * sine).astype(jnp.bfloat16)

        kv_ref[c, core, y, row, :ROWS, :] = turned(total[:, :HD])
        kv_ref[c, core, y, row, ROWS:TAG, :] = total[:, HD : 2 * HD].astype(jnp.bfloat16)
        tag = ids_ref[0, c // 2].astype(jnp.float32)
        kv_ref[c, core, y, row, TAG:, :] = jnp.full((16, HD), tag, jnp.float32).astype(jnp.bfloat16)
        rows_at[c] = key_rows(c)
        for head in range(4):
            at = head * SPAN + (c % 2) * ROWS
            q_ref[c // 2, at : at + ROWS, :] = turned(total[:, (2 + head) * HD : (3 + head) * HD])

    def side_step(c):
        sides_at[c] = key_sides(c, rows_at[c])

    def forward_step(c):
        moved_at[c] = key_forwards(c, sides_at[c])

    def last_step(c):
        mates.extend(key_last(c, moved_at[c]))

    for c in range(CHUNKS):
        own_of[c] = side_sends(c, 0)
        across_of[c] = across_send(c)
    actions = {
        "n": near_step,
        "a": across_step,
        "f": far_step,
        "d": multiply,
        "x": finish,
        "s": side_step,
        "w": forward_step,
        "l": last_step,
    }
    for action in ORDER:
        if action == "d0":
            for load in loads[1:]:
                load.wait()
        actions[action[0]](int(action[1:]))
    for copy in mates:
        copy.wait_recv()
    for copy in sent:
        copy.wait_send()
    for c in range(CHUNKS):
        out = rows_at[c][0]
        out[1].wait_send()
        pl.when(row != 3)(out[0].wait_send)
        pl.when(row != 0)(out[2].wait_send)
        pl.when(inner)(sides_at[c][2].wait_send)


def project(span_ids, positions, tokens, q_weight, k_weight, v_weight):
    vmem = pl.BlockSpec(memory_space=pltpu.VMEM)
    hbm = pl.BlockSpec(memory_space=pltpu.HBM)
    return pl.pallas_call(
        project_kernel,
        out_shape=(
            jax.ShapeDtypeStruct((2, 4 * SPAN, HD), jnp.bfloat16),
            jax.ShapeDtypeStruct((CHUNKS, 2, 4, 4, BLOCK, HD), jnp.bfloat16),
        ),
        in_specs=[hbm] * 6,
        out_specs=(vmem, vmem),
        scratch_shapes=[
            pltpu.SMEM(span_ids.shape, jnp.int32),
            pltpu.VMEM(positions.shape, jnp.int32),
            pltpu.VMEM(tokens.shape, jnp.bfloat16),
            pltpu.VMEM(q_weight.shape, jnp.bfloat16),
            pltpu.VMEM(k_weight.shape, jnp.bfloat16),
            pltpu.VMEM(v_weight.shape, jnp.bfloat16),
            pltpu.VMEM((2, 4) + tokens.shape, jnp.bfloat16),
            pltpu.SemaphoreType.DMA((6,)),
            pltpu.SemaphoreType.DMA((CHUNKS * TOKEN_SEMS,)),
            pltpu.SemaphoreType.DMA((CHUNKS * TOKEN_SEMS,)),
            pltpu.SemaphoreType.DMA((CHUNKS * KEY_SEMS,)),
            pltpu.SemaphoreType.DMA((CHUNKS * KEY_SEMS,)),
        ],
        compiler_params=pltpu.CompilerParams(
            collective_id=0, has_side_effects=True, vmem_limit_bytes=26 * 1024 * 1024
        ),
        name="project",
    )(
        *(
            pltpu.with_memory_space_constraint(array, pltpu.HBM)
            for array in (span_ids, positions, tokens, q_weight, k_weight, v_weight)
        )
    )


WIDTHS = (4, 2, 1)


def attend_kernel(
    ids_hbm, positions_hbm, q_ref, kv_ref, out_ref, ids, places_of, positions_ref, top_ref, acc_ref,
    start_ref, table_ref, where, sems,
):
    loads = [
        pltpu.make_async_copy(a, b, sems.at[i + 1])
        for i, (a, b) in enumerate(
            ((ids_hbm, ids), (positions_hbm, positions_ref), (positions_hbm, places_of))
        )
    ]
    for load in loads:
        load.start()
    heads = q_ref.shape[1] // SPAN
    scale = LOG2E * HD**-0.5
    ones = jnp.ones((SPAN, HD), jnp.bfloat16)
    lane = lax.broadcasted_iota(jnp.int32, (8, 128), 1).astype(jnp.float32)
    table = jnp.zeros((8, 128), jnp.int32)
    for block in range(64):
        at = (block // 32) * 64 + block % 32
        tag = kv_ref[at, TAG:, :].astype(jnp.float32)[:8]
        table = table + jnp.where(tag == lane, block, 0)
    table_ref[...] = table
    fetch = pltpu.make_async_copy(table_ref, where, sems.at[0])
    fetch.start()
    row, y, core = lax.axis_index("cp_0"), lax.axis_index("cp_1"), lax.axis_index("cp_2")
    home = core * 16 + y * 4 + row
    for load in loads:
        load.wait()
    for half in range(2):
        own = ids[0, half]
        for part in range(2):
            line = 2 * half + part
            column = columns_of(positions_ref[line : line + 1, :].astype(jnp.float32))
            place = own * SPAN + part * 128
            place = place + lax.broadcasted_iota(jnp.int32, (128, 128), 0)
            start_ref[half, part * 128 : (part + 1) * 128, :] = place - column.astype(jnp.int32)

    def block(half, span, places_in, masked, first):
        places = []
        for place in places_in:
            first_place = (place // 32) * 64 + lax.rem(place, 32)
            places += [first_place, first_place + 32]
        wide = 2 * len(places_in)
        keys = jnp.concatenate([kv_ref[at, :ROWS, :] for at in places], axis=0)
        values = jnp.concatenate([kv_ref[at, ROWS:TAG, :] for at in places], axis=0)
        values = jnp.concatenate([values, jnp.concatenate([ones] * len(places_in), axis=0)], axis=1)
        if masked:
            key = span * SPAN + lax.broadcasted_iota(jnp.int32, (SPAN, SPAN), 1)
            start = start_ref[half]
            seen = key >= jnp.concatenate([start, start], axis=1)
            if first:
                query = span * SPAN + lax.broadcasted_iota(jnp.int32, (SPAN, SPAN), 0)
                seen = seen & (key <= query)
        for head in range(heads):
            rows = slice(head * SPAN, (head + 1) * SPAN)
            score = lax.dot_general(
                q_ref[half, rows, :],
                keys,
                (((1,), (1,)), ((), ())),
                preferred_element_type=jnp.float32,
            )
            score = score * scale
            if masked:
                score = jnp.where(seen, score, floor_score)
            top = jnp.max(score, axis=1, keepdims=True)
            if first:
                weight = jnp.exp2(score - top)
                top_ref[half, rows, :] = jnp.broadcast_to(top, (SPAN, HD))
            else:
                before = top_ref[half, rows, :]
                now = jnp.maximum(before, top)
                weight = jnp.exp2(score - jnp.concatenate([now] * wide, axis=1))
                fade = jnp.exp2(before - now)
                top_ref[half, rows, :] = now
            mixed = jnp.dot(
                weight.astype(jnp.bfloat16), values, preferred_element_type=jnp.float32
            )
            if not first:
                mixed = mixed + acc_ref[half, rows, :] * jnp.concatenate([fade, fade], axis=1)
            acc_ref[half, rows, :] = mixed

    for half in range(2):
        block(half, ids[0, half], (home + 32 * half,), True, True)
    fetch.wait()
    for half in range(2):
        own = ids[0, half]
        low = (own * SPAN - places_of[2 * half, 0]) // SPAN
        clear = (own * SPAN + 2 * SPAN - 2 - places_of[2 * half + 1, 127]) // SPAN
        clear = jnp.minimum(clear, own)

        def masked_step(span, carry):
            block(half, span, (where[0, span],), True, False)
            return carry

        def clear_steps(begin, count):
            def step(i, carry):
                at = begin + i * count
                block(half, None, [where[0, at + j] for j in range(count)], False, False)
                return carry

            steps = (own - begin) // count
            lax.fori_loop(0, steps, step, 0)
            return begin + steps * count

        lax.fori_loop(low, clear, masked_step, 0)
        for count in WIDTHS:
            clear = clear_steps(clear, count)
        for head in range(heads):
            rows = slice(head * SPAN, (head + 1) * SPAN)
            mixed = acc_ref[half, rows, :HD] / acc_ref[half, rows, HD:]
            out_ref[half * SPAN : (half + 1) * SPAN, head * HD : (head + 1) * HD] = mixed.astype(
                jnp.bfloat16
            )


def attend(span_ids, positions, queries, held):
    vmem = pl.BlockSpec(memory_space=pltpu.VMEM)
    hbm = pl.BlockSpec(memory_space=pltpu.HBM)
    rows = queries.shape[1]
    heads = rows // SPAN
    return pl.pallas_call(
        attend_kernel,
        out_shape=jax.ShapeDtypeStruct((2 * SPAN, heads * HD), jnp.bfloat16),
        in_specs=[hbm, hbm, vmem, vmem],
        out_specs=vmem,
        scratch_shapes=[
            pltpu.SMEM(span_ids.shape, jnp.int32),
            pltpu.SMEM(positions.shape, jnp.int32),
            pltpu.VMEM(positions.shape, jnp.int32),
            pltpu.VMEM((2, rows, HD), jnp.float32),
            pltpu.VMEM((2, rows, 2 * HD), jnp.float32),
            pltpu.VMEM((2, SPAN, HD), jnp.int32),
            pltpu.VMEM((8, 128), jnp.int32),
            pltpu.SMEM((8, 128), jnp.int32),
            pltpu.SemaphoreType.DMA((4,)),
        ],
        compiler_params=pltpu.CompilerParams(vmem_limit_bytes=20 * 1024 * 1024),
        name="attend",
    )(
        *(pltpu.with_memory_space_constraint(array, pltpu.HBM) for array in (span_ids, positions)),
        queries,
        held,
    )


def combine_kernel(
    attn_ref, weight_ref, out_ref, far_out, far_in, near_out, near_in, over_out, over_in, kept,
    send_sem, recv_sem,
):
    x, zhi = lax.axis_index("tp_1"), lax.axis_index("tp_0")
    right, left, across = shifted(x=1), shifted(x=-1), shifted(z=1)
    greet([right, left, across])
    sems = (send_sem, recv_sem)
    steps = kept.shape[0]
    size = kept.shape[1]
    half = size // 2
    width = out_ref.shape[1]
    sent = []

    def share(c, dx):
        rows = attn_ref[c * size : (c + 1) * size, :]
        terms = []
        for dz in range(2):
            owner = lax.rem(zhi + dz, 2) * 4 + lax.rem(x + dx, 4)
            columns = pl.ds(pl.multiple_of(owner * width, width), width)
            terms.append(
                jnp.dot(rows, weight_ref[:, columns], preferred_element_type=jnp.float32)
            )
        return jnp.concatenate(terms, axis=1)

    def open_step(c):
        far = share(c, 2).astype(jnp.bfloat16)
        far_out[c, 0] = far[:half]
        far_out[c, 1] = far[half:]
        a = send(far_out.at[c, 0], far_in.at[c, 0], sems, c * 7, right)
        b = send(far_out.at[c, 1], far_in.at[c, 1], sems, c * 7 + 1, left)
        to_right, to_left = share(c, 1), share(c, 3)
        near_out[c, 0, 1] = to_right[half:].astype(jnp.bfloat16)
        d = send(near_out.at[c, 0, 1], near_in.at[c, 0, 1], sems, c * 7 + 2, right)
        near_out[c, 1, 0] = to_left[:half].astype(jnp.bfloat16)
        e = send(near_out.at[c, 1, 0], near_in.at[c, 1, 0], sems, c * 7 + 3, left)
        near_out[c, 0, 0] = to_right[:half].astype(jnp.bfloat16)
        near_out[c, 1, 1] = to_left[half:].astype(jnp.bfloat16)
        sent.extend((a, b, d, e))
        return a, b, d, e

    def pass_on(c, opened):
        a, b, d, e = opened
        a.wait_recv()
        near_out[c, 0, 0] = (
            near_out[c, 0, 0].astype(jnp.float32) + far_in[c, 0].astype(jnp.float32)
        ).astype(jnp.bfloat16)
        f = send(near_out.at[c, 0, 0], near_in.at[c, 0, 0], sems, c * 7 + 4, right)
        b.wait_recv()
        near_out[c, 1, 1] = (
            near_out[c, 1, 1].astype(jnp.float32) + far_in[c, 1].astype(jnp.float32)
        ).astype(jnp.bfloat16)
        g = send(near_out.at[c, 1, 1], near_in.at[c, 1, 1], sems, c * 7 + 5, left)
        sent.extend((f, g))
        return d, e, f, g

    def cross(c, passed):
        total = share(c, 0)
        for copy in passed:
            copy.wait_recv()
        for side in range(2):
            both = jnp.concatenate([near_in[c, side, 0], near_in[c, side, 1]], axis=0)
            total = total + both.astype(jnp.float32)
        over_out[c] = total[:, width:].astype(jnp.bfloat16)
        kept[c] = total[:, :width]
        copy = send(over_out.at[c], over_in.at[c], sems, c * 7 + 6, across)
        sent.append(copy)
        return copy

    def close(c, crossed):
        crossed.wait_recv()
        out_ref[c * size : (c + 1) * size, :] = (
            kept[c] + over_in[c].astype(jnp.float32)
        ).astype(jnp.bfloat16)

    opened, passed, crossed = {}, {}, {}
    for c in range(2):
        opened[c] = open_step(c)
    for c in range(steps):
        passed[c] = pass_on(c, opened[c])
        if c + 2 < steps:
            opened[c + 2] = open_step(c + 2)
        if c >= 1:
            crossed[c - 1] = cross(c - 1, passed[c - 1])
        if c >= 2:
            close(c - 2, crossed[c - 2])
    crossed[steps - 1] = cross(steps - 1, passed[steps - 1])
    close(steps - 2, crossed[steps - 2])
    close(steps - 1, crossed[steps - 1])
    for copy in sent:
        copy.wait_send()


STEPS = 4


def combine(attention, o_weight):
    vmem = pl.BlockSpec(memory_space=pltpu.VMEM)
    rows, width = attention.shape[0], o_weight.shape[1] // 8
    size = rows // STEPS
    half = (size // 2, 2 * width)
    return pl.pallas_call(
        combine_kernel,
        out_shape=jax.ShapeDtypeStruct((rows, width), jnp.bfloat16),
        in_specs=[vmem, vmem],
        out_specs=vmem,
        scratch_shapes=[
            pltpu.VMEM((STEPS, 2) + half, jnp.bfloat16),
            pltpu.VMEM((STEPS, 2) + half, jnp.bfloat16),
            pltpu.VMEM((STEPS, 2, 2) + half, jnp.bfloat16),
            pltpu.VMEM((STEPS, 2, 2) + half, jnp.bfloat16),
            pltpu.VMEM((STEPS, size, width), jnp.bfloat16),
            pltpu.VMEM((STEPS, size, width), jnp.bfloat16),
            pltpu.VMEM((STEPS, size, width), jnp.float32),
            pltpu.SemaphoreType.DMA((STEPS * 7,)),
            pltpu.SemaphoreType.DMA((STEPS * 7,)),
        ],
        compiler_params=pltpu.CompilerParams(
            collective_id=1, has_side_effects=True, vmem_limit_bytes=32 * 1024 * 1024
        ),
        name="combine",
    )(attention, o_weight)


def per_device(tokens, span_ids, positions, q_weight, k_weight, v_weight, o_weight):
    lines = positions.reshape(CHUNKS, ROWS)
    queries, held = project(span_ids, lines, tokens, q_weight, k_weight, v_weight)
    attention = attend(span_ids, lines, queries, held.reshape(-1, BLOCK, HD))
    return combine(attention, o_weight)


def solution(mesh):
    split = Mesh(mesh.devices.reshape(4, 4, 2, 2, 4), ("cp_0", "cp_1", "cp_2", "tp_0", "tp_1"))
    placed = (P(CP, TP), P(CP, None), P(CP), P(None, TP), P(None, TP), P(None, TP), P(TP, None))
    return jax.shard_map(
        per_device, mesh=split, in_specs=placed, out_specs=P(CP, TP), check_vma=False
    )
```

```python
import jax
import jax.numpy as jnp
from jax import lax
from jax.experimental import pallas as pl
from jax.experimental.pallas import tpu as pltpu
from jax.sharding import Mesh
from jax.sharding import PartitionSpec as P

HD = 128
SPAN = 256
LOG2E = 1.4426950408889634
TP = ("tp_0", "tp_1")
CP = ("cp_0", "cp_1", "cp_2")


theta_base = 500000.0
floor_score = -1e30


MESH = pl.DeviceIdType.MESH
CHUNKS = 4
ROWS = 128
TAG = 2 * ROWS
BLOCK = TAG + 16


def shifted(x=0, y=0, z=0, row=0, other_core=False):
    place = {}
    if x:
        place["tp_1"] = lax.rem(lax.axis_index("tp_1") + x + 4, 4)
    if y:
        place["cp_1"] = lax.rem(lax.axis_index("cp_1") + y + 4, 4)
    if z:
        place["tp_0"] = 1 - lax.axis_index("tp_0")
    if row:
        place["cp_0"] = lax.rem(lax.axis_index("cp_0") + row + 4, 4)
    if other_core:
        place["cp_2"] = 1 - lax.axis_index("cp_2")
    return place


def greet(peers):
    barrier = pltpu.get_barrier_semaphore()
    for peer in peers:
        pl.semaphore_signal(barrier, inc=1, device_id=peer, device_id_type=MESH)
    pl.semaphore_wait(barrier, len(peers))


def sending(source, target, sems, index, peer, arrival=None):
    return pltpu.make_async_remote_copy(
        src_ref=source,
        dst_ref=target,
        send_sem=sems[0].at[index],
        recv_sem=sems[1].at[index if arrival is None else arrival],
        device_id=peer,
        device_id_type=MESH,
    )


def send(source, target, sems, index, peer):
    copy = sending(source, target, sems, index, peer)
    copy.start()
    return copy


def columns_of(line):
    return jnp.broadcast_to(line, (128, 128)).T


def turn_table(line):
    lane = lax.rem(lax.broadcasted_iota(jnp.int32, (8, 128), 1), HD // 2)
    frequency = jnp.zeros((8, 128), jnp.float32)
    for j in range(HD // 2):
        frequency = jnp.where(lane == j, theta_base ** (-2.0 * j / HD), frequency)
    angle = columns_of(line.astype(jnp.float32)) * frequency[:1]
    turns = jnp.floor(angle * 0.6366197723675814 + 0.5)
    rest = ((angle - turns * 1.5703125) - turns * 4.837512969970703e-4) - turns * 7.549789954891882e-8
    square = rest * rest
    cosine = (2.443315711809948e-5 * square - 1.388731625493765e-3) * square + 4.166664568298827e-2
    cosine = cosine * square * square - 0.5 * square + 1.0
    sine = (-1.9515295891e-4 * square + 8.3321608736e-3) * square - 1.6666654611e-1
    sine = sine * square * rest + rest
    quarter = turns - 4.0 * jnp.floor(turns * 0.25)
    odd = (quarter == 1.0) | (quarter == 3.0)
    cos_all = jnp.where(odd, sine, cosine)
    sin_all = jnp.where(odd, cosine, sine)
    cos_all = jnp.where((quarter == 1.0) | (quarter == 2.0), -cos_all, cos_all)
    sin_all = jnp.where(quarter >= 2.0, -sin_all, sin_all)
    side = lax.broadcasted_iota(jnp.int32, (128, 128), 1)
    return cos_all, jnp.where(side < HD // 2, -sin_all, sin_all)


ORDER = (
    "n0", "a0", "n1", "f0", "a1", "d0", "x0", "n2", "f1", "n3",
    "a2", "d1", "x1", "s0", "f2", "a3", "d2", "x2", "s1", "w0",
    "f3", "d3", "l0", "x3", "s2", "w1", "s3", "w2", "l1", "w3",
    "l2", "l3",
)
TOKEN_SEMS = 9
KEY_SEMS = 20


def project_kernel(
    ids_hbm,
    positions_hbm,
    tokens_hbm,
    wq_hbm,
    wk_hbm,
    wv_hbm,
    q_ref,
    kv_ref,
    ids_ref,
    positions_ref,
    tokens_ref,
    wq_ref,
    wk_ref,
    wv_ref,
    held,
    load_sem,
    token_send,
    token_recv,
    key_send,
    key_recv,
):
    x, zhi = lax.axis_index("tp_1"), lax.axis_index("tp_0")
    row, y, core = lax.axis_index("cp_0"), lax.axis_index("cp_1"), lax.axis_index("cp_2")
    loads = [
        pltpu.make_async_copy(a, b, load_sem.at[i])
        for i, (a, b) in enumerate(
            (
                (tokens_hbm, tokens_ref),
                (ids_hbm, ids_ref),
                (positions_hbm, positions_ref),
                (wk_hbm, wk_ref),
                (wv_hbm, wv_ref),
                (wq_hbm, wq_ref),
            )
        )
    ]
    for load in loads:
        load.start()
    right, left, across = shifted(x=1), shifted(x=-1), shifted(z=1)
    up, down, mate = shifted(y=1), shifted(y=-1), shifted(other_core=True)
    rows_of = [shifted(row=d) for d in (1, 2, 3)]
    greet([right, left, across, up, down, mate] + rows_of)
    tok, key = (token_send, token_recv), (key_send, key_recv)
    sent = []
    half = ROWS // 2
    inner = (row == 1) | (row == 2)
    loads[0].wait()

    def token_rows(c, part=None):
        if part is None:
            return pl.ds(c * ROWS, ROWS)
        return pl.ds(c * ROWS + part * half, half)

    def across_send(c):
        rows = token_rows(c)
        copy = send(
            tokens_ref.at[rows], held.at[1, 0, rows], tok, c * TOKEN_SEMS + 8, across
        )
        sent.append(copy)
        return copy

    def side_sends(c, dz):
        rows = token_rows(c)
        source = held.at[1, 0, rows] if dz else tokens_ref.at[rows]
        a = send(source, held.at[dz, 3, rows], tok, c * TOKEN_SEMS + dz * 4, right)
        b = send(source, held.at[dz, 1, rows], tok, c * TOKEN_SEMS + dz * 4 + 1, left)
        sent.extend((a, b))
        return a, b

    def side_forwards(c, dz):
        at = c * TOKEN_SEMS + dz * 4
        rows = token_rows(c, 0)
        a = send(held.at[dz, 3, rows], held.at[dz, 2, rows], tok, at + 2, right)
        rows = token_rows(c, 1)
        b = send(held.at[dz, 1, rows], held.at[dz, 2, rows], tok, at + 3, left)
        sent.extend((a, b))
        return a, b

    def product(c, dz, dx):
        owner = lax.rem(zhi + dz, 2) * 4 + lax.rem(x + dx, 4)
        rows = pl.ds(pl.multiple_of(owner * 512, 512), 512)
        weights = jnp.concatenate([wk_ref[rows, :], wv_ref[rows, :], wq_ref[rows, :]], axis=1)
        if dz == 0 and dx == 0:
            features = tokens_ref[token_rows(c), :]
        else:
            features = held[dz, dx, token_rows(c), :]
        return jnp.dot(features, weights, preferred_element_type=jnp.float32)

    def key_rows(c):
        at = c * KEY_SEMS
        block = kv_ref.at[c, core, y, row]
        out = []
        for d, skip in ((1, row == 3), (2, None), (3, row == 0)):
            copy = sending(block, block, key, at + d - 1, rows_of[d - 1])
            if skip is None:
                copy.start()
            else:
                pl.when(jnp.logical_not(skip))(copy.start)
            out.append(copy)
        return out, [key_side(c, 0)]

    def key_side(c, d):
        block = kv_ref.at[c, core, y, lax.rem(row + 4 - d, 4)]
        a = send(block, block, key, c * KEY_SEMS + 4 + d, up)
        b = send(block, block, key, c * KEY_SEMS + 8 + d, down)
        sent.extend((a, b))
        return a, b

    def key_relay(c):
        at = c * KEY_SEMS
        block = kv_ref.at[c, core, y, lax.rem(row + 2, 4)]
        end = {"cp_0": jnp.where(row == 2, 3, 0)}
        arrival = at + jnp.where(row == 2, 2, 0)
        return sending(block, block, key, at + 3, end, arrival)

    def key_sides(c, started):
        out, sides = started
        relay = key_relay(c)
        out[1].wait_recv()
        pl.when(inner)(relay.start)
        sides.append(key_side(c, 2))
        out[0].wait_recv()
        sides.append(key_side(c, 1))
        out[2].wait_recv()
        sides.append(key_side(c, 3))
        mine = kv_ref.at[c, core, y]
        m = send(mine, mine, key, c * KEY_SEMS + 16, mate)
        sent.append(m)
        return sides, m, relay

    def key_forwards(c, state):
        sides, m, relay = state
        at = c * KEY_SEMS
        behind, ahead = lax.rem(y + 3, 4), lax.rem(y + 1, 4)
        forwards = []
        for place, d in enumerate((0, 2, 1, 3)):
            a, b = sides[place]
            block_at = lax.rem(row + 4 - d, 4)
            a.wait_recv()
            b.wait_recv()
            if d in (0, 1):
                block = kv_ref.at[c, core, behind, block_at]
                f = send(block, block, key, at + 12 + d, up)
            else:
                block = kv_ref.at[c, core, ahead, block_at]
                f = send(block, block, key, at + 12 + d, down)
            forwards.append(f)
        mates = [m]
        for i, at_y in enumerate((behind, ahead)):
            got = kv_ref.at[c, core, at_y]
            mates.append(send(got, got, key, at + 17 + i, mate))
        sent.extend(forwards + mates[1:])
        return forwards, mates

    def key_last(c, moved):
        forwards, mates = moved
        for f in forwards:
            f.wait_recv()
        got = kv_ref.at[c, core, lax.rem(y + 2, 4)]
        mc = send(got, got, key, c * KEY_SEMS + 19, mate)
        sent.append(mc)
        return mates + [mc]

    across_of, own_of, far_of, near_on, far_on = {}, {}, {}, {}, {}
    rows_at, sides_at, moved_at, totals, mates = {}, {}, {}, {}, []

    def near_step(c):
        for copy in own_of[c]:
            copy.wait_recv()
        near_on[c] = side_forwards(c, 0)

    def across_step(c):
        if c < CHUNKS:
            across_of[c].wait_recv()
            far_of[c] = side_sends(c, 1)

    def far_step(c):
        if c < CHUNKS:
            for copy in far_of[c]:
                copy.wait_recv()
            far_on[c] = side_forwards(c, 1)

    def multiply(c):
        total = product(c, 0, 0)
        for dz, dx in ((0, 3), (0, 1), (1, 0), (1, 3), (1, 1)):
            total = total + product(c, dz, dx)
        totals[c] = total

    def finish(c):
        total = totals[c]
        cosine, sine = turn_table(positions_ref[c : c + 1, :])
        for copy in near_on[c]:
            copy.wait_recv()
        total = total + product(c, 0, 2)
        for copy in far_on[c]:
            copy.wait_recv()
        total = total + product(c, 1, 2)

        def turned(vectors):
            return (vectors * cosine + pltpu.roll(vectors, HD // 2, 1) * sine).astype(jnp.bfloat16)

        kv_ref[c, core, y, row, :ROWS, :] = turned(total[:, :HD])
        kv_ref[c, core, y, row, ROWS:TAG, :] = total[:, HD : 2 * HD].astype(jnp.bfloat16)
        tag = ids_ref[0, c // 2].astype(jnp.float32)
        kv_ref[c, core, y, row, TAG:, :] = jnp.full((16, HD), tag, jnp.float32).astype(jnp.bfloat16)
        rows_at[c] = key_rows(c)
        for head in range(4):
            at = head * SPAN + (c % 2) * ROWS
            q_ref[c // 2, at : at + ROWS, :] = turned(total[:, (2 + head) * HD : (3 + head) * HD])

    def side_step(c):
        sides_at[c] = key_sides(c, rows_at[c])

    def forward_step(c):
        moved_at[c] = key_forwards(c, sides_at[c])

    def last_step(c):
        mates.extend(key_last(c, moved_at[c]))

    for c in range(CHUNKS):
        own_of[c] = side_sends(c, 0)
        across_of[c] = across_send(c)
    actions = {
        "n": near_step,
        "a": across_step,
        "f": far_step,
        "d": multiply,
        "x": finish,
        "s": side_step,
        "w": forward_step,
        "l": last_step,
    }
    for action in ORDER:
        if action == "d0":
            for load in loads[1:]:
                load.wait()
        actions[action[0]](int(action[1:]))
    for copy in mates:
        copy.wait_recv()
    for copy in sent:
        copy.wait_send()
    for c in range(CHUNKS):
        out = rows_at[c][0]
        out[1].wait_send()
        pl.when(row != 3)(out[0].wait_send)
        pl.when(row != 0)(out[2].wait_send)
        pl.when(inner)(sides_at[c][2].wait_send)


def project(span_ids, positions, tokens, q_weight, k_weight, v_weight):
    vmem = pl.BlockSpec(memory_space=pltpu.VMEM)
    hbm = pl.BlockSpec(memory_space=pltpu.HBM)
    return pl.pallas_call(
        project_kernel,
        out_shape=(
            jax.ShapeDtypeStruct((2, 4 * SPAN, HD), jnp.bfloat16),
            jax.ShapeDtypeStruct((CHUNKS, 2, 4, 4, BLOCK, HD), jnp.bfloat16),
        ),
        in_specs=[hbm] * 6,
        out_specs=(vmem, vmem),
        scratch_shapes=[
            pltpu.SMEM(span_ids.shape, jnp.int32),
            pltpu.VMEM(positions.shape, jnp.int32),
            pltpu.VMEM(tokens.shape, jnp.bfloat16),
            pltpu.VMEM(q_weight.shape, jnp.bfloat16),
            pltpu.VMEM(k_weight.shape, jnp.bfloat16),
            pltpu.VMEM(v_weight.shape, jnp.bfloat16),
            pltpu.VMEM((2, 4) + tokens.shape, jnp.bfloat16),
            pltpu.SemaphoreType.DMA((6,)),
            pltpu.SemaphoreType.DMA((CHUNKS * TOKEN_SEMS,)),
            pltpu.SemaphoreType.DMA((CHUNKS * TOKEN_SEMS,)),
            pltpu.SemaphoreType.DMA((CHUNKS * KEY_SEMS,)),
            pltpu.SemaphoreType.DMA((CHUNKS * KEY_SEMS,)),
        ],
        compiler_params=pltpu.CompilerParams(
            collective_id=0, has_side_effects=True, vmem_limit_bytes=26 * 1024 * 1024
        ),
        name="project",
    )(
        *(
            pltpu.with_memory_space_constraint(array, pltpu.HBM)
            for array in (span_ids, positions, tokens, q_weight, k_weight, v_weight)
        )
    )


WIDTHS = (4, 2, 1)


def attend_kernel(
    ids_hbm, positions_hbm, q_ref, kv_ref, out_ref, ids, places_of, positions_ref, top_ref, acc_ref,
    start_ref, table_ref, where, sems,
):
    loads = [
        pltpu.make_async_copy(a, b, sems.at[i + 1])
        for i, (a, b) in enumerate(
            ((ids_hbm, ids), (positions_hbm, positions_ref), (positions_hbm, places_of))
        )
    ]
    for load in loads:
        load.start()
    heads = q_ref.shape[1] // SPAN
    scale = LOG2E * HD**-0.5
    ones = jnp.ones((SPAN, HD), jnp.bfloat16)
    lane = lax.broadcasted_iota(jnp.int32, (8, 128), 1).astype(jnp.float32)
    table = jnp.zeros((8, 128), jnp.int32)
    for block in range(64):
        at = (block // 32) * 64 + block % 32
        tag = kv_ref[at, TAG:, :].astype(jnp.float32)[:8]
        table = table + jnp.where(tag == lane, block, 0)
    table_ref[...] = table
    fetch = pltpu.make_async_copy(table_ref, where, sems.at[0])
    fetch.start()
    row, y, core = lax.axis_index("cp_0"), lax.axis_index("cp_1"), lax.axis_index("cp_2")
    home = core * 16 + y * 4 + row
    for load in loads:
        load.wait()
    for half in range(2):
        own = ids[0, half]
        for part in range(2):
            line = 2 * half + part
            column = columns_of(positions_ref[line : line + 1, :].astype(jnp.float32))
            place = own * SPAN + part * 128
            place = place + lax.broadcasted_iota(jnp.int32, (128, 128), 0)
            start_ref[half, part * 128 : (part + 1) * 128, :] = place - column.astype(jnp.int32)

    def block(half, span, places_in, masked, first):
        places = []
        for place in places_in:
            first_place = (place // 32) * 64 + lax.rem(place, 32)
            places += [first_place, first_place + 32]
        wide = 2 * len(places_in)
        keys = jnp.concatenate([kv_ref[at, :ROWS, :] for at in places], axis=0)
        values = jnp.concatenate([kv_ref[at, ROWS:TAG, :] for at in places], axis=0)
        values = jnp.concatenate([values, jnp.concatenate([ones] * len(places_in), axis=0)], axis=1)
        if masked:
            key = span * SPAN + lax.broadcasted_iota(jnp.int32, (SPAN, SPAN), 1)
            start = start_ref[half]
            seen = key >= jnp.concatenate([start, start], axis=1)
            if first:
                query = span * SPAN + lax.broadcasted_iota(jnp.int32, (SPAN, SPAN), 0)
                seen = seen & (key <= query)
        for head in range(heads):
            rows = slice(head * SPAN, (head + 1) * SPAN)
            score = lax.dot_general(
                q_ref[half, rows, :],
                keys,
                (((1,), (1,)), ((), ())),
                preferred_element_type=jnp.float32,
            )
            score = score * scale
            if masked:
                score = jnp.where(seen, score, floor_score)
            top = jnp.max(score, axis=1, keepdims=True)
            if first:
                weight = jnp.exp2(score - top)
                top_ref[half, rows, :] = jnp.broadcast_to(top, (SPAN, HD))
            else:
                before = top_ref[half, rows, :]
                now = jnp.maximum(before, top)
                weight = jnp.exp2(score - jnp.concatenate([now] * wide, axis=1))
                fade = jnp.exp2(before - now)
                top_ref[half, rows, :] = now
            mixed = jnp.dot(
                weight.astype(jnp.bfloat16), values, preferred_element_type=jnp.float32
            )
            if not first:
                mixed = mixed + acc_ref[half, rows, :] * jnp.concatenate([fade, fade], axis=1)
            acc_ref[half, rows, :] = mixed

    for half in range(2):
        block(half, ids[0, half], (home + 32 * half,), True, True)
    fetch.wait()
    for half in range(2):
        own = ids[0, half]
        low = (own * SPAN - places_of[2 * half, 0]) // SPAN
        clear = (own * SPAN + 2 * SPAN - 2 - places_of[2 * half + 1, 127]) // SPAN
        clear = jnp.minimum(clear, own)

        def masked_step(span, carry):
            block(half, span, (where[0, span],), True, False)
            return carry

        def clear_steps(begin, count):
            def step(i, carry):
                at = begin + i * count
                block(half, None, [where[0, at + j] for j in range(count)], False, False)
                return carry

            steps = (own - begin) // count
            lax.fori_loop(0, steps, step, 0)
            return begin + steps * count

        lax.fori_loop(low, clear, masked_step, 0)
        for count in WIDTHS:
            clear = clear_steps(clear, count)
        for head in range(heads):
            rows = slice(head * SPAN, (head + 1) * SPAN)
            mixed = acc_ref[half, rows, :HD] / acc_ref[half, rows, HD:]
            out_ref[half * SPAN : (half + 1) * SPAN, head * HD : (head + 1) * HD] = mixed.astype(
                jnp.bfloat16
            )


def attend(span_ids, positions, queries, held):
    vmem = pl.BlockSpec(memory_space=pltpu.VMEM)
    hbm = pl.BlockSpec(memory_space=pltpu.HBM)
    rows = queries.shape[1]
    heads = rows // SPAN
    return pl.pallas_call(
        attend_kernel,
        out_shape=jax.ShapeDtypeStruct((2 * SPAN, heads * HD), jnp.bfloat16),
        in_specs=[hbm, hbm, vmem, vmem],
        out_specs=vmem,
        scratch_shapes=[
            pltpu.SMEM(span_ids.shape, jnp.int32),
            pltpu.SMEM(positions.shape, jnp.int32),
            pltpu.VMEM(positions.shape, jnp.int32),
            pltpu.VMEM((2, rows, HD), jnp.float32),
            pltpu.VMEM((2, rows, 2 * HD), jnp.float32),
            pltpu.VMEM((2, SPAN, HD), jnp.int32),
            pltpu.VMEM((8, 128), jnp.int32),
            pltpu.SMEM((8, 128), jnp.int32),
            pltpu.SemaphoreType.DMA((4,)),
        ],
        compiler_params=pltpu.CompilerParams(vmem_limit_bytes=20 * 1024 * 1024),
        name="attend",
    )(
        *(pltpu.with_memory_space_constraint(array, pltpu.HBM) for array in (span_ids, positions)),
        queries,
        held,
    )


STEPS = 8
COMBINE_ORDER = (
    "o0", "o1", "o2", "o3", "p0", "o4", "p1", "c0", "o5", "p2",
    "c1", "o6", "p3", "c2", "o7", "p4", "c3", "e0", "p5", "c4",
    "e1", "p6", "c5", "e2", "p7", "c6", "e3", "c7", "e4", "e5",
    "e6", "e7",
)


def combine_kernel(
    attn_ref, weight_ref, out_ref, far_out, far_in, near_out, near_in, over_out, over_in, kept,
    send_sem, recv_sem,
):
    x, zhi = lax.axis_index("tp_1"), lax.axis_index("tp_0")
    right, left, across = shifted(x=1), shifted(x=-1), shifted(z=1)
    greet([right, left, across])
    sems = (send_sem, recv_sem)
    steps = kept.shape[0]
    size = kept.shape[1]
    half = size // 2
    width = out_ref.shape[1]
    sent = []

    def share(c, dx):
        rows = attn_ref[c * size : (c + 1) * size, :]
        terms = []
        for dz in range(2):
            owner = lax.rem(zhi + dz, 2) * 4 + lax.rem(x + dx, 4)
            columns = pl.ds(pl.multiple_of(owner * width, width), width)
            terms.append(
                jnp.dot(rows, weight_ref[:, columns], preferred_element_type=jnp.float32)
            )
        return jnp.concatenate(terms, axis=1)

    def open_step(c):
        far = share(c, 2).astype(jnp.bfloat16)
        far_out[c, 0] = far[:half]
        far_out[c, 1] = far[half:]
        a = send(far_out.at[c, 0], far_in.at[c, 0], sems, c * 7, right)
        b = send(far_out.at[c, 1], far_in.at[c, 1], sems, c * 7 + 1, left)
        to_right, to_left = share(c, 1), share(c, 3)
        near_out[c, 0, 1] = to_right[half:].astype(jnp.bfloat16)
        d = send(near_out.at[c, 0, 1], near_in.at[c, 0, 1], sems, c * 7 + 2, right)
        near_out[c, 1, 0] = to_left[:half].astype(jnp.bfloat16)
        e = send(near_out.at[c, 1, 0], near_in.at[c, 1, 0], sems, c * 7 + 3, left)
        near_out[c, 0, 0] = to_right[:half].astype(jnp.bfloat16)
        near_out[c, 1, 1] = to_left[half:].astype(jnp.bfloat16)
        sent.extend((a, b, d, e))
        return a, b, d, e

    def pass_on(c, opened):
        a, b, d, e = opened
        a.wait_recv()
        near_out[c, 0, 0] = (
            near_out[c, 0, 0].astype(jnp.float32) + far_in[c, 0].astype(jnp.float32)
        ).astype(jnp.bfloat16)
        f = send(near_out.at[c, 0, 0], near_in.at[c, 0, 0], sems, c * 7 + 4, right)
        b.wait_recv()
        near_out[c, 1, 1] = (
            near_out[c, 1, 1].astype(jnp.float32) + far_in[c, 1].astype(jnp.float32)
        ).astype(jnp.bfloat16)
        g = send(near_out.at[c, 1, 1], near_in.at[c, 1, 1], sems, c * 7 + 5, left)
        sent.extend((f, g))
        return d, e, f, g

    def cross(c, passed):
        total = share(c, 0)
        for copy in passed:
            copy.wait_recv()
        for side in range(2):
            both = jnp.concatenate([near_in[c, side, 0], near_in[c, side, 1]], axis=0)
            total = total + both.astype(jnp.float32)
        over_out[c] = total[:, width:].astype(jnp.bfloat16)
        kept[c] = total[:, :width]
        copy = send(over_out.at[c], over_in.at[c], sems, c * 7 + 6, across)
        sent.append(copy)
        return copy

    def close(c, crossed):
        crossed.wait_recv()
        out_ref[c * size : (c + 1) * size, :] = (
            kept[c] + over_in[c].astype(jnp.float32)
        ).astype(jnp.bfloat16)

    opened, passed, crossed = {}, {}, {}
    for action in COMBINE_ORDER:
        c = int(action[1])
        if action[0] == "o":
            opened[c] = open_step(c)
        elif action[0] == "p":
            passed[c] = pass_on(c, opened[c])
        elif action[0] == "c":
            crossed[c] = cross(c, passed[c])
        else:
            close(c, crossed[c])
    for copy in sent:
        copy.wait_send()


def combine(attention, o_weight):
    vmem = pl.BlockSpec(memory_space=pltpu.VMEM)
    rows, width = attention.shape[0], o_weight.shape[1] // 8
    size = rows // STEPS
    half = (size // 2, 2 * width)
    return pl.pallas_call(
        combine_kernel,
        out_shape=jax.ShapeDtypeStruct((rows, width), jnp.bfloat16),
        in_specs=[vmem, vmem],
        out_specs=vmem,
        scratch_shapes=[
            pltpu.VMEM((STEPS, 2) + half, jnp.bfloat16),
            pltpu.VMEM((STEPS, 2) + half, jnp.bfloat16),
            pltpu.VMEM((STEPS, 2, 2) + half, jnp.bfloat16),
            pltpu.VMEM((STEPS, 2, 2) + half, jnp.bfloat16),
            pltpu.VMEM((STEPS, size, width), jnp.bfloat16),
            pltpu.VMEM((STEPS, size, width), jnp.bfloat16),
            pltpu.VMEM((STEPS, size, width), jnp.float32),
            pltpu.SemaphoreType.DMA((STEPS * 7,)),
            pltpu.SemaphoreType.DMA((STEPS * 7,)),
        ],
        compiler_params=pltpu.CompilerParams(
            collective_id=1, has_side_effects=True, vmem_limit_bytes=32 * 1024 * 1024
        ),
        name="combine",
    )(attention, o_weight)


def per_device(tokens, span_ids, positions, q_weight, k_weight, v_weight, o_weight):
    lines = positions.reshape(CHUNKS, ROWS)
    queries, held = project(span_ids, lines, tokens, q_weight, k_weight, v_weight)
    attention = attend(span_ids, lines, queries, held.reshape(-1, BLOCK, HD))
    return combine(attention, o_weight)


def solution(mesh):
    split = Mesh(mesh.devices.reshape(4, 4, 2, 2, 4), ("cp_0", "cp_1", "cp_2", "tp_0", "tp_1"))
    placed = (P(CP, TP), P(CP, None), P(CP), P(None, TP), P(None, TP), P(None, TP), P(TP, None))
    return jax.shard_map(
        per_device, mesh=split, in_specs=placed, out_specs=P(CP, TP), check_vma=False
    )
```
